32 devices in a mesh: rhombus: 4 (over z), tile: 8 (over y, x, core).
Axes of the slice: x: 2, y: 2, z: 4, core: 2. Of those that a mesh axis runs over, the one named last changes fastest.
Arguments:
- fine_latent: bfloat16 [16384, 512], P(('rhombus', 'tile')), may hold values from -6 to 6
- mid_latent: bfloat16 [1024, 512], P(('rhombus', 'tile')), may hold values from -6 to 6
- coarse_latent: bfloat16 [642, 512], replicated, may hold values from -6 to 6
- fine_parent: int32 [16384], P(('rhombus', 'tile')), may hold values from 0 to 95, as said below
- mid_parent: int32 [1024], P(('rhombus', 'tile')), may hold values from 0 to 641
- halo_rows: int32 [8192], P(('rhombus', 'tile')), may hold values from 0 to 511
- edge_source: int32 [98304], P(('rhombus', 'tile')), may hold values from 0 to 767
- edge_target: int32 [98304], P(('rhombus', 'tile')), may hold values from 0 to 512, as said below
- w_child: bfloat16 [512, 512], replicated, may hold values from -1 to 1
- mid_w1: bfloat16 [512, 512], replicated, may hold values from -0.25 to 0.25
- mid_w2: bfloat16 [512, 512], replicated, may hold values from -0.5 to 0.5
- mid_w3: bfloat16 [512, 512], replicated, may hold values from -0.25 to 0.25
- w_coarse: bfloat16 [512, 512], replicated, may hold values from -1 to 1
- coarse_w1: bfloat16 [512, 512], replicated, may hold values from -0.25 to 0.25
- coarse_w2: bfloat16 [512, 512], replicated, may hold values from -0.5 to 0.5
- coarse_w3: bfloat16 [512, 512], replicated, may hold values from -0.25 to 0.25
- w_descend: bfloat16 [512, 512], replicated, may hold values from -0.25 to 0.25
- w_fine: bfloat16 [512, 512], replicated, may hold values from -0.25 to 0.25
- edge_w_src: bfloat16 [512, 512], replicated, may hold values from -1 to 1
- edge_w_dst: bfloat16 [512, 512], replicated, may hold values from -0.25 to 0.25
- edge_w2: bfloat16 [512, 512], replicated, may hold values from -0.25 to 0.25
- node_w1: bfloat16 [512, 512], replicated, may hold values from -0.25 to 0.25
- node_w2: bfloat16 [512, 512], replicated, may hold values from -0.125 to 0.125
- node_w3: bfloat16 [512, 512], replicated, may hold values from -0.25 to 0.25
Outputs:
- fine_out: bfloat16 [16384, 512], P(('rhombus', 'tile'))
- mid_out: bfloat16 [1024, 512], P(('rhombus', 'tile'))
- coarse_out: bfloat16 [642, 512], replicated
The draws below stay inside these ranges and needn't reach their ends.
Inputs may be any that keep to these rules, and one draw needn't show every extreme that they name: `fine_parent`: in tile t of a group, an entry p < 32 names a middle slot of the same tile, 32 <= p < 64 a slot of tile t - 1, 64 <= p a slot of tile t + 1; tile 0 never names the tile before and the last tile of a group never names the tile after. `edge_target`: in each tile the live slots come first and name a fine row of that tile; the remaining slots hold 512. Each tile has at least 1536 live slots, and some tile has all 3072 slots live.
All inputs are finite; a program needn't handle non-finite values.
Results may differ from the reference program's by a relative error of at most 0.013.
Values may be sent and summed in bfloat16 or wider, within the bound.
A program may use at most 64 MiB of HBM per device.

```python
import jax
import jax.numpy as jnp
from jax import lax

D = 512
HIDDEN_SIZE = 512
FINE_DEV = 512
MID_DEV = 32
HALO = 128
EDGES_DEV = 3072
COARSE = 642
GROUPS = 4
TILES = 8
FINE = 16384
MIDS = 1024


def draw_fine_parent(key, part):
    first_key, second_key = jax.random.split(jax.random.fold_in(key, 11))
    total = GROUPS * TILES * FINE_DEV
    side = jax.random.randint(first_key, (total,), 0, 8)
    within = jax.random.randint(second_key, (total,), 0, MID_DEV)
    tile_of = jnp.arange(total, dtype=jnp.int32) // FINE_DEV % TILES
    before = (side == 0) & (tile_of > 0)
    after = (side == 1) & (tile_of < TILES - 1)
    return jnp.where(before, within + MID_DEV, jnp.where(after, within + 2 * MID_DEV, within)).astype(jnp.int32)


def draw_mid_parent(key, part):
    near_key, far_key, pick_key = jax.random.split(jax.random.fold_in(key, 37), 3)
    blocks = GROUPS * TILES
    total = blocks * MID_DEV
    block_of = jnp.arange(total, dtype=jnp.int32) // MID_DEV
    start = block_of * COARSE // blocks
    offset = jax.random.randint(near_key, (total,), 0, 3)
    nearby = (start + offset) % COARSE
    anywhere = jax.random.randint(far_key, (total,), 0, COARSE)
    pick = jax.random.randint(pick_key, (total,), 0, 4)
    return jnp.where(pick == 0, anywhere, nearby).astype(jnp.int32)


def draw_edge_target(key, part):
    live_key, full_key, target_key = jax.random.split(jax.random.fold_in(key, 23), 3)
    blocks = GROUPS * TILES
    live = jax.random.randint(live_key, (blocks,), EDGES_DEV // 2, EDGES_DEV + 1)
    fullest = jax.random.randint(full_key, (), 0, blocks)
    live = jnp.where(jnp.arange(blocks, dtype=jnp.int32) == fullest, EDGES_DEV, live)
    slot_ids = jnp.arange(EDGES_DEV, dtype=jnp.int32)
    target = jax.random.randint(target_key, (blocks, EDGES_DEV), 0, FINE_DEV)
    marked = jnp.where(slot_ids[None, :] < live[:, None], target, FINE_DEV)
    return marked.reshape(blocks * EDGES_DEV).astype(jnp.int32)


def flat_map(key, marker, row_count, column_count, factor):
    widest = max(row_count, column_count)
    noise_key, sign_key = jax.random.split(jax.random.fold_in(key, marker))
    noise_draw = jnp.clip(jax.random.normal(noise_key, (widest, widest), jnp.float32), -4.0, 4.0)
    spread = 0.4
    skewed = (noise_draw - noise_draw.T) / jnp.sqrt(2.0 * widest)
    square = jnp.eye(widest, dtype=jnp.float32) + spread * skewed
    sign_flip = (2 * jax.random.randint(sign_key, (widest,), 0, 2) - 1).astype(jnp.float32)
    return (factor * square * sign_flip[None, :])[:row_count, :column_count]


def draw_w_child(key, part):
    return flat_map(key, 51, D, D, 1.0).astype(jnp.bfloat16)


def draw_mid_w2(key, part):
    return flat_map(key, 53, D, HIDDEN_SIZE, 0.5).astype(jnp.bfloat16)


def draw_w_coarse(key, part):
    return flat_map(key, 57, D, D, 1.0).astype(jnp.bfloat16)


def draw_coarse_w2(key, part):
    return flat_map(key, 59, D, HIDDEN_SIZE, 0.5).astype(jnp.bfloat16)


def draw_edge_w_src(key, part):
    return flat_map(key, 61, D, HIDDEN_SIZE, 1.0).astype(jnp.bfloat16)


def set_ends(drawn, key, smallest, top_value):
    shape = drawn.shape
    spot = [jax.random.randint(jax.random.fold_in(key, axis), (), 0, shape[axis]) for axis in range(len(shape))]
    drawn = drawn.at[tuple(spot)].set(smallest)
    longest = shape.index(max(shape))
    spot[longest] = (spot[longest] + 1) % shape[longest]
    return drawn.at[tuple(spot)].set(top_value)


def block_scale(own_key, shape, pieces, least, largest):
    level = 1.0
    for position, parts in pieces:
        steps = jax.random.uniform(jax.random.fold_in(jax.random.fold_in(own_key, 6), position), (parts,), jnp.float32, least / len(pieces), largest / len(pieces))
        level = level * jnp.repeat(jnp.exp(steps), shape[position] // parts).reshape((-1,) + (1,) * (len(shape) - 1 - position))
    return level


def normal_values(stream_key, dims, width, most, cuts=(), kind=jnp.bfloat16):
    values = jax.random.normal(stream_key, dims, jnp.float32) * width
    if len(cuts) > 0:
        values = block_scale(stream_key, dims, cuts, -0.22, 0.18) * values
    return jnp.clip(values, min=-most, max=most).astype(kind)


def setup_inputs(seed: int = 0) -> dict:
    splits = jax.random.split(jax.random.key(seed), 25)
    fine_latent = normal_values(splits[0], (FINE, D), 1.0, 6.0, ((0, 32),))
    mid_latent = normal_values(splits[1], (MIDS, D), 1.0, 6.0, ((0, 32),))
    coarse_latent = normal_values(splits[2], (COARSE, D), 1.0, 6.0)
    fine_parent = draw_fine_parent(jax.random.fold_in(splits[24], 71), 0)
    mid_parent = draw_mid_parent(jax.random.fold_in(splits[24], 71), 0)
    halo_rows = set_ends(jax.random.randint(splits[5], (FINE // 2,), 0, FINE_DEV), jax.random.fold_in(splits[5], 1), 0, FINE_DEV - 1).astype(jnp.int32)
    edge_source = set_ends(jax.random.randint(splits[6], (FINE * 6,), 0, FINE_DEV + 2 * HALO), jax.random.fold_in(splits[6], 1), 0, (FINE_DEV + 2 * HALO) - 1).astype(jnp.int32)
    edge_target = draw_edge_target(jax.random.fold_in(splits[24], 71), 0)
    w_child = draw_w_child(jax.random.fold_in(splits[24], 71), 0)
    mid_w1 = normal_values(splits[9], (D, HIDDEN_SIZE), D ** -0.5, 0.25)
    mid_w2 = draw_mid_w2(jax.random.fold_in(splits[24], 71), 0)
    mid_w3 = normal_values(splits[11], (HIDDEN_SIZE, D), HIDDEN_SIZE ** -0.5, 0.25)
    w_coarse = draw_w_coarse(jax.random.fold_in(splits[24], 71), 0)
    coarse_w1 = normal_values(splits[13], (D, HIDDEN_SIZE), D ** -0.5, 0.25)
    coarse_w2 = draw_coarse_w2(jax.random.fold_in(splits[24], 71), 0)
    coarse_w3 = normal_values(splits[15], (HIDDEN_SIZE, D), HIDDEN_SIZE ** -0.5, 0.25)
    w_descend = normal_values(splits[16], (D, D), D ** -0.5, 0.25)
    w_fine = normal_values(splits[17], (D, D), D ** -0.5, 0.25)
    edge_w_src = draw_edge_w_src(jax.random.fold_in(splits[24], 71), 0)
    edge_w_dst = normal_values(splits[19], (D, HIDDEN_SIZE), D ** -0.5, 0.25)
    edge_w2 = normal_values(splits[20], (HIDDEN_SIZE, D), HIDDEN_SIZE ** -0.5, 0.25)
    node_w1 = normal_values(splits[21], (D, HIDDEN_SIZE), D ** -0.5, 0.25)
    node_w2 = normal_values(splits[22], (D, HIDDEN_SIZE), (4 * D) ** -0.5, 0.125)
    node_w3 = normal_values(splits[23], (HIDDEN_SIZE, D), HIDDEN_SIZE ** -0.5, 0.25)
    return dict(fine_latent=fine_latent, mid_latent=mid_latent, coarse_latent=coarse_latent, fine_parent=fine_parent, mid_parent=mid_parent, halo_rows=halo_rows, edge_source=edge_source, edge_target=edge_target, w_child=w_child, mid_w1=mid_w1, mid_w2=mid_w2, mid_w3=mid_w3, w_coarse=w_coarse, coarse_w1=coarse_w1, coarse_w2=coarse_w2, coarse_w3=coarse_w3, w_descend=w_descend, w_fine=w_fine, edge_w_src=edge_w_src, edge_w_dst=edge_w_dst, edge_w2=edge_w2, node_w1=node_w1, node_w2=node_w2, node_w3=node_w3)


EPSILON = 1e-05

def product(left, right):
    return jnp.dot(left, right, preferred_element_type=jnp.float32)

def normed(values):
    return values / jnp.sqrt(lax.optimization_barrier(jnp.mean(values * values, axis=-1, keepdims=True)) + EPSILON)

def node_update(latent, incoming, first, second, third):
    hidden = jax.nn.silu(product(latent, first) + product(incoming, second)).astype(jnp.bfloat16)
    return (latent.astype(jnp.float32) + normed(product(hidden, third))).astype(jnp.bfloat16)

def edge_update(node_table, lifted, source, target, edge_w_src, edge_w_dst, edge_w2, node_w1, node_w2, node_w3):
    fine_count = lifted.shape[0]
    sender = product(node_table, edge_w_src).astype(jnp.bfloat16)
    receiver = product(lifted, edge_w_dst).astype(jnp.bfloat16)
    receiver = jnp.concatenate([receiver, jnp.zeros((1, receiver.shape[1]), jnp.bfloat16)], axis=0)
    edge_sum = jnp.take(sender, source, axis=0).astype(jnp.float32) + jnp.take(receiver, target, axis=0).astype(jnp.float32)
    edge_hidden = jax.nn.silu(edge_sum).astype(jnp.bfloat16)
    message = product(edge_hidden, edge_w2)
    aggregate = jax.ops.segment_sum(message, target, num_segments=fine_count + 1)[:fine_count]
    return node_update(lifted, aggregate.astype(jnp.bfloat16), node_w1, node_w2, node_w3)

def take_rows(node_block, row_ids):
    return jnp.take(node_block, row_ids, axis=0)

def reference(fine_latent, mid_latent, coarse_latent, fine_parent, mid_parent, halo_rows, edge_source, edge_target, w_child, mid_w1, mid_w2, mid_w3, w_coarse, coarse_w1, coarse_w2, coarse_w3, w_descend, w_fine, edge_w_src, edge_w_dst, edge_w2, node_w1, node_w2, node_w3):
    blocks = GROUPS * TILES
    fine_block = (jnp.arange(blocks * FINE_DEV, dtype=jnp.int32) // FINE_DEV).astype(jnp.int32)
    parent_side = (fine_parent // MID_DEV).astype(jnp.int32)
    offset = jnp.where(parent_side == 1, -1, jnp.where(parent_side == 2, 1, 0)).astype(jnp.int32)
    parent_index = ((fine_block + offset) * MID_DEV + fine_parent % MID_DEV).astype(jnp.int32)
    child_msg = product(fine_latent, w_child).astype(jnp.bfloat16)
    mid_in = jax.ops.segment_sum(child_msg.astype(jnp.float32), parent_index, num_segments=blocks * MID_DEV)
    mid_up = node_update(mid_latent, mid_in.astype(jnp.bfloat16), mid_w1, mid_w2, mid_w3)
    mid_msg = product(mid_up, w_coarse).astype(jnp.bfloat16)
    coarse_in = jax.ops.segment_sum(mid_msg.astype(jnp.float32), mid_parent, num_segments=COARSE)
    coarse_out = node_update(coarse_latent, coarse_in.astype(jnp.bfloat16), coarse_w1, coarse_w2, coarse_w3)
    down_coarse = product(coarse_out, w_descend).astype(jnp.bfloat16)
    mid_out = (mid_up.astype(jnp.float32) + jnp.take(down_coarse, mid_parent, axis=0).astype(jnp.float32)).astype(jnp.bfloat16)
    fine_down = product(mid_out, w_fine).astype(jnp.bfloat16)
    lifted = (fine_latent.astype(jnp.float32) + jnp.take(fine_down, parent_index, axis=0).astype(jnp.float32)).astype(jnp.bfloat16)
    features = lifted.shape[1]
    lifted_blocks = lifted.reshape(GROUPS, TILES, FINE_DEV, features)
    chosen = halo_rows.reshape(GROUPS, TILES, 2 * HALO)
    boundary = jax.vmap(jax.vmap(take_rows))(lifted_blocks, chosen)
    empty = jnp.zeros((GROUPS, 1, HALO, features), jnp.bfloat16)
    from_before = jnp.concatenate([empty, boundary[:, :-1, HALO:]], axis=1)
    from_after = jnp.concatenate([boundary[:, 1:, :HALO], empty], axis=1)
    node_table = jnp.concatenate([lifted_blocks, from_before, from_after], axis=2).reshape(blocks, FINE_DEV + 2 * HALO, features)

    def one_block(packed):
        return edge_update(packed[0], packed[1], packed[2], packed[3], edge_w_src, edge_w_dst, edge_w2, node_w1, node_w2, node_w3)
    fine_out = lax.map(one_block, (node_table, lifted_blocks.reshape(blocks, FINE_DEV, features), edge_source.reshape(blocks, EDGES_DEV), edge_target.reshape(blocks, EDGES_DEV)))
    return (fine_out.reshape(blocks * FINE_DEV, features), mid_out, coarse_out)
```

```python
import jax
import jax.numpy as jnp
from jax import lax
from jax.experimental import pallas as pl
from jax.experimental.pallas import tpu as pltpu
from jax.sharding import PartitionSpec as P

MESH = pl.DeviceIdType.MESH

EPSILON = 1e-05

bf16, f32, i32 = (jnp.bfloat16, jnp.float32, jnp.int32)

ACROSS = (((1,), (1,)), ((), ()))


def product(left, right):
    return jnp.dot(left, right, preferred_element_type=f32)


def flipped(left, right):
    return lax.dot_general(left, right, ACROSS, preferred_element_type=f32)


def normed(values):
    return values / jnp.sqrt(jnp.mean(values * values, axis=-1, keepdims=True) + EPSILON)


def gate(values):
    return values * (0.5 + 0.5 * jnp.tanh(0.5 * values))


def one_hot(ids, axis, shape):
    return jnp.where(lax.broadcasted_iota(i32, shape, axis) == ids, 1.0, 0.0).astype(bf16)


def as_columns(row, width):
    count = row.shape[1]
    column = jnp.transpose(jnp.broadcast_to(row, (128, count)))
    return jnp.concatenate([column] * (width // 128), axis=1)


def ceil(n, unit=128):
    return -(-n // unit) * unit


GATHER_WEIGHTS = (
    "w_child",
    "mid_w2",
    "mid_w1",
    "mid_w3",
    "w_coarse",
    "coarse_w2",
    "edge_w_dst",
    "edge_w_src",
    "coarse_w1",
    "edge_w2",
    "node_w2",
)
FINISH_WEIGHTS = ("node_w1", "coarse_w3", "w_descend", "w_fine", "node_w3")
SMALL = ("parent", "halo", "coarse_id", "latent", "source", "target")


def gather_kernel(groups, tiles, *refs):
    refs = iter(refs)

    def take(n):
        return [next(refs) for _ in range(n)]

    small_refs = dict(zip(SMALL, take(len(SMALL))))
    fine_ref, coarse_ref = take(2)
    weight_refs = dict(zip(GATHER_WEIGHTS + FINISH_WEIGHTS, take(len(GATHER_WEIGHTS + FINISH_WEIGHTS))))
    pre_v, known_v, lookup_v, target_v, first_v, fine_v, coarse_v = take(7)
    near_v, pick_v, lift_v, flip_v, ending_v, handed_v = take(6)
    ups_ref, ids_ref, rim_ref, rim_parent_ref, weights_v = take(5)
    small_v = dict(zip(SMALL, take(len(SMALL))))
    side_v, beside_v, picked_v, picked_parent_v, table_v = take(5)
    load_sem, near_send, near_recv, tree_send, block_recv, id_recv = take(6)

    group, tile = (lax.axis_index("rhombus"), lax.axis_index("tile"))
    pairs = tiles // 2
    pair, core = (tile // 2, tile % 2)
    mids = small_v["latent"].shape[0]
    rims = small_v["halo"].shape[1] // 2
    fines, features = fine_v.shape
    coarse_count = coarse_v.shape[0]
    edges = small_v["source"].shape[1]

    def at(group_id, pair_id, core_id):
        return (group_id, pair_id * 2 + core_id)

    columns = [at((group + k) % groups, pair, core) for k in range(1, groups)]
    if pairs == 4:
        level = [pair + 1 - 2 * (pair % 2), (pair + 2) % 4]
        corner = (level[0] + 2) % 4
    else:
        level = [(pair + k) % pairs for k in range(1, pairs)]
    row_peers = [at(group, other, core) for other in level]
    partner = at(group, pair, 1 - core)
    peers = columns + row_peers + [partner]

    barrier = pltpu.get_barrier_semaphore()
    for peer in peers:
        pl.semaphore_signal(barrier, inc=1, device_id=peer, device_id_type=MESH)

    @pl.when(tile > 0)
    def _():
        pl.semaphore_signal(barrier, inc=1, device_id=(group, tile - 1), device_id_type=MESH)

    @pl.when(tile < tiles - 1)
    def _():
        pl.semaphore_signal(barrier, inc=1, device_id=(group, tile + 1), device_id_type=MESH)

    loads = {}

    def load(name, source, held):
        loads[name] = pltpu.make_async_copy(source, held, load_sem.at[len(loads)])
        loads[name].start()

    load("parent", small_refs["parent"], small_v["parent"])
    load("fine", fine_ref, fine_v)
    for name in ("halo", "latent", "coarse_id"):
        load(name, small_refs[name], small_v[name])
    held = {name: weights_v.at[i] for i, name in enumerate(GATHER_WEIGHTS)}
    held.update({name: handed_v.at[i] for i, name in enumerate(FINISH_WEIGHTS)})
    for name in GATHER_WEIGHTS[:8]:
        load(name, weight_refs[name], held[name])
    for name in ("source", "target"):
        load(name, small_refs[name], small_v[name])
    load("coarse", coarse_ref, coarse_v)
    for name in GATHER_WEIGHTS[8:] + FINISH_WEIGHTS:
        load(name, weight_refs[name], held[name])

    def weight(name):
        loads[name].wait()
        return held[name][...]

    me = group * tiles + tile
    halves = groups * pairs

    def place_of(group_id, pair_id, core_id):
        return core_id * halves + group_id * pairs + pair_id

    mine = place_of(group, pair, core)
    loads["parent"].wait()
    parents = small_v["parent"][...]
    picker = one_hot(parents, 0, (3 * mids, fines))
    loads["fine"].wait()
    sums = product(picker, fine_v[...])
    side_v[0] = sums[mids : 2 * mids].astype(bf16)
    side_v[1] = sums[2 * mids :].astype(bf16)
    pl.semaphore_wait(barrier, len(peers) + 1 + (tile + tiles - 1) // tiles - (tile + 1) // tiles)

    def near(index, source, target, device):
        return pltpu.make_async_remote_copy(
            src_ref=source,
            dst_ref=target,
            send_sem=near_send.at[index],
            recv_sem=near_recv.at[index],
            device_id=device,
            device_id_type=MESH,
        )

    before, after = ((group, tile - 1), (group, tile + 1))
    to_before = [
        near(0, side_v.at[0], beside_v.at[0], before),
        near(1, picked_v.at[pl.ds(0, rims)], rim_ref.at[pl.ds(rims, rims)], before),
        near(2, picked_parent_v.at[0], rim_parent_ref.at[1], before),
    ]
    to_after = [
        near(3, side_v.at[1], beside_v.at[1], after),
        near(4, picked_v.at[pl.ds(rims, rims)], rim_ref.at[pl.ds(0, rims)], after),
        near(5, picked_parent_v.at[1], rim_parent_ref.at[0], after),
    ]

    @pl.when(tile > 0)
    def _():
        to_before[0].start()

    @pl.when(tile < tiles - 1)
    def _():
        to_after[0].start()

    loads["halo"].wait()
    halo = small_v["halo"][...]
    picked_v[...] = product(one_hot(as_columns(halo, fines), 1, (2 * rims, fines)), fine_v[...]).astype(bf16)
    side = parents // mids
    shift = jnp.where(side == 1, -1, jnp.where(side == 2, 1, 0))
    within = parents % mids
    parent_column = jnp.transpose(jnp.broadcast_to((me + shift) * mids + within, (128, fines)))
    for half in range(2):
        hit = lax.broadcasted_iota(i32, (fines, rims), 0) == halo[:, half * rims : (half + 1) * rims]
        spread = jnp.concatenate([parent_column] * (rims // 128), axis=1)
        picked_parent_v[half] = jnp.sum(jnp.where(hit, spread, 0), axis=0, keepdims=True)

    @pl.when(tile > 0)
    def _():
        to_before[1].start()
        to_before[2].start()

    @pl.when(tile < tiles - 1)
    def _():
        to_after[1].start()
        to_after[2].start()

    child_mid = product(weight("w_child"), weight("mid_w2")).astype(bf16)
    loads["latent"].wait()
    kept_mid = product(small_v["latent"][...], weight("mid_w1"))
    loads["coarse_id"].wait()
    spare_ids = jnp.zeros((1, ids_ref.shape[2] - mids), i32)
    ids_ref[mine] = jnp.concatenate([small_v["coarse_id"][...], spare_ids], axis=1)
    msg_coarse = product(weight("w_coarse"), weight("coarse_w2")).astype(bf16)
    flip_v[1] = jnp.transpose(weight("edge_w_dst"))
    table_v[:features, fines + 2 * rims :] = flipped(flip_v[1], fine_v[...]).astype(bf16)
    flip_v[0] = jnp.transpose(weight("edge_w_src"))
    table_v[:features, :fines] = flipped(flip_v[0], fine_v[...]).astype(bf16)
    mid_w3 = weight("mid_w3")

    @pl.when(tile > 0)
    def _():
        to_after[0].wait_recv()

    @pl.when(tile == 0)
    def _():
        beside_v[1] = jnp.zeros_like(beside_v[1])
        rim_ref[pl.ds(0, rims)] = jnp.zeros((rims, features), bf16)
        rim_parent_ref[0] = jnp.full(rim_parent_ref.shape[1:], -1, i32)

    @pl.when(tile < tiles - 1)
    def _():
        to_before[0].wait_recv()

    @pl.when(tile == tiles - 1)
    def _():
        beside_v[0] = jnp.zeros_like(beside_v[0])
        rim_ref[pl.ds(rims, rims)] = jnp.zeros((rims, features), bf16)
        rim_parent_ref[1] = jnp.full(rim_parent_ref.shape[1:], -1, i32)

    total = (sums[:mids] + beside_v[0].astype(f32) + beside_v[1].astype(f32)).astype(bf16)
    hidden = gate(kept_mid + product(total, child_mid)).astype(bf16)
    mid_up = small_v["latent"][...].astype(f32) + normed(product(hidden, mid_w3))
    ups_ref[mine] = mid_up.astype(bf16)

    started = []

    def copies(slot, index, device):
        return [
            pltpu.make_async_remote_copy(
                src_ref=held.at[slot],
                dst_ref=held.at[slot],
                send_sem=tree_send.at[kind, index],
                recv_sem=sems.at[slot],
                device_id=device,
                device_id_type=MESH,
            )
            for kind, (held, sems) in enumerate([(ups_ref, block_recv), (ids_ref, id_recv)])
        ]

    def send(slot, devices):
        for device in devices:
            for copy in copies(slot, len(started) // 2, device):
                copy.start()
                started.append(copy)

    def arrive(slot):
        for copy in copies(slot, 0, partner):
            copy.wait_recv()

    def slot_of(k, pair_id, core_id):
        return place_of((group + k) % groups, pair_id, core_id)

    order = [0] + sorted(range(1, groups), key=lambda k: min(k, groups - k))
    send(mine, columns + row_peers + [partner])

    def keep_coarse():
        loads["coarse"].wait()
        pre_v[...] = product(coarse_v[...], weight("coarse_w1"))

    def keep_ending():
        ending_v[...] = product(weight("edge_w2"), weight("node_w2")).astype(bf16)

    def keep_first():
        first_v[...] = product(fine_v[...], weight("node_w1"))

    own_near = (1 + shift) * mids + within

    def fill_table():
        @pl.when(tile > 0)
        def _():
            for copy in to_after[1:]:
                copy.wait_recv()

        @pl.when(tile < tiles - 1)
        def _():
            for copy in to_before[1:]:
                copy.wait_recv()

        table_v[:features, fines : fines + 2 * rims] = flipped(flip_v[0], rim_ref[...]).astype(bf16)
        far = jnp.concatenate([rim_parent_ref[0], rim_parent_ref[1]], axis=1)
        far = jnp.where(far < 0, -1, far - (me - 2) * mids)
        blank = jnp.zeros((1, fines), i32)
        source_parent = jnp.concatenate([own_near + mids, far, blank], axis=1)
        target_parent = jnp.concatenate([blank, jnp.zeros((1, 2 * rims), i32), own_near], axis=1)
        line = lax.broadcasted_iota(i32, (table_v.shape[0] - features, table_v.shape[1]), 0)
        named = jnp.where(line == 0, source_parent, jnp.where(line == 1, target_parent, 0))
        table_v[features:] = named.astype(f32).astype(bf16)
        lift_v[...] = one_hot(as_columns(own_near, lift_v.shape[1]), 1, lift_v.shape)

    step = next(size for size in (512, 256, 128) if edges % size == 0)

    def known(i):
        span = pl.ds(i * step, step)
        source_pick = one_hot(small_v["source"][:, span], 0, (fines + 2 * rims, step))
        target_pick = one_hot(small_v["target"][:, span], 0, (fines, step))
        target_v[:, span] = target_pick
        found = product(table_v[...], jnp.concatenate([source_pick, target_pick], axis=0))
        known_v[:, span] = found[:features].astype(bf16)
        source_near = found[features : features + 1].astype(i32)
        target_near = found[features + 1 : features + 2].astype(i32) + 5 * mids
        line = lax.broadcasted_iota(i32, (8 * mids, step), 0)
        lookup_v[:, span] = jnp.where((line == source_near) | (line == target_near), 1.0, 0.0).astype(bf16)

    def load_edges():
        loads["source"].wait()
        loads["target"].wait()

    work = [keep_coarse, keep_ending, keep_first, fill_table, load_edges]
    work += [lambda i=i: known(i) for i in range(edges // step)]

    def do(n):
        for _ in range(min(n, len(work))):
            work.pop(0)()

    def coarse_part(slots):
        blocks = jnp.concatenate([ups_ref[slot] for slot in slots], axis=0)
        id_row = jnp.concatenate([ids_ref[slot][:, :mids] for slot in slots], axis=1)
        told = product(blocks, msg_coarse).astype(bf16)
        pre_v[...] += product(one_hot(id_row, 0, (coarse_count, len(slots) * mids)), told)

    do(4)
    for k in order:
        if k > 0:
            slot = slot_of(k, pair, core)
            arrive(slot)
            send(slot, row_peers + [partner])
    if pairs == 4:
        for n, k in enumerate(order):
            do(2 if n == 0 else 1)
            for place, other in enumerate(level):
                slot = slot_of(k, other, core)
                arrive(slot)
                onward = [partner]
                if n % 2 == place:
                    onward = [at(group, level[1 - place], core), partner]
                send(slot, onward)
        do(1)
        for k in order:
            slot = slot_of(k, corner, core)
            arrive(slot)
            send(slot, [partner])
        do(len(work))
        for k in order:
            arrive(slot_of(k, pair, 1 - core))
        coarse_part([slot_of(k, pair, c) for c in (core, 1 - core) for k in order])
        coarse_part([slot_of(k, other, core) for other in level for k in order])
        for other in level:
            for k in order:
                arrive(slot_of(k, other, 1 - core))
        coarse_part([slot_of(k, other, 1 - core) for other in level for k in order])
        for k in order:
            arrive(slot_of(k, corner, 1 - core))
        coarse_part([slot_of(k, corner, c) for c in (core, 1 - core) for k in order])
    else:
        for k in order:
            for other in level:
                slot = slot_of(k, other, core)
                arrive(slot)
                send(slot, [partner])
        do(len(work))
        for k in order:
            for other in range(pairs):
                arrive(slot_of(k, other, 1 - core))
        batch = next(size for size in (8, 4, 2, 1) if 2 * halves % size == 0)

        def part(i, carry):
            coarse_part([i * batch + j for j in range(batch)])
            return carry

        lax.fori_loop(0, 2 * halves // batch, part, 0)

    nearby = []
    for d in range(-2, 3):
        other = (me + d + 2 * groups * tiles) % (groups * tiles)
        other_tile = other % tiles
        nearby.append(place_of(other // tiles, other_tile // 2, other_tile % 2))
    window, padded = pick_v.shape
    spare = ceil(window) - window
    near_row = jnp.concatenate([ids_ref[slot][:, :mids] for slot in nearby] + [jnp.zeros((1, spare), i32)], axis=1)
    pick_v[...] = one_hot(as_columns(near_row, padded)[:window], 1, (window, padded))
    near_v[...] = jnp.concatenate([ups_ref[slot] for slot in nearby], axis=0)

    @pl.when(tile > 0)
    def _():
        for copy in to_before:
            copy.wait_send()

    @pl.when(tile < tiles - 1)
    def _():
        for copy in to_after:
            copy.wait_send()

    for copy in started:
        copy.wait_send()
    for name in FINISH_WEIGHTS[1:]:
        loads[name].wait()


def finish_kernel(*refs):
    pre_v, known_v, lookup_v, target_v, first_v, fine_v, coarse_v = refs[:7]
    near_v, pick_v, lift_v, flip_v, ending_v, handed_v = refs[7:13]
    fine_out_ref, mid_out_ref, coarse_out_ref = refs[13:16]
    fine_out_v, mid_out_v, coarse_out_v, padded_v, sums_v, out_sem = refs[16:]
    window, padded = pick_v.shape
    mids = mid_out_v.shape[0]
    fines, features = fine_v.shape
    coarse_count = coarse_v.shape[0]
    edges = known_v.shape[1]
    weights = {name: handed_v.at[i] for i, name in enumerate(FINISH_WEIGHTS)}
    outs = []

    def put(source, target):
        outs.append(pltpu.make_async_copy(source, target, out_sem.at[len(outs)]))
        outs[-1].start()

    hidden = gate(pre_v[...]).astype(bf16)
    updated = (coarse_v[...].astype(f32) + normed(product(hidden, weights["coarse_w3"][...]))).astype(bf16)
    coarse_out_v[...] = updated
    put(coarse_out_v, coarse_out_ref)
    edge = coarse_count // 16 * 16
    padded_v[edge:] = jnp.zeros((padded - edge, features), bf16)
    padded_v[:coarse_count] = updated

    picked = product(pick_v[...], padded_v[...]).astype(bf16)
    down = product(picked, weights["w_descend"][...])
    near_out = (near_v[...].astype(f32) + down).astype(bf16)
    mid_out_v[...] = near_out[2 * mids : 3 * mids]
    put(mid_out_v, mid_out_ref)
    fine_down = product(near_out, weights["w_fine"][...]).astype(bf16)
    beside = fine_down[mids : 4 * mids]

    def blank(rows):
        return jnp.zeros((rows, features), bf16)

    source_rows = jnp.concatenate([fine_down, blank(3 * mids)], axis=0)
    target_rows = jnp.concatenate([blank(5 * mids), beside], axis=0)
    change = (flipped(flip_v[0], source_rows) + flipped(flip_v[1], target_rows)).astype(bf16)

    step = next(size for size in (1024, 512, 256, 128) if edges % size == 0)
    total = None
    for i in range(edges // step):
        span = slice(i * step, (i + 1) * step)
        edge_sum = product(change, lookup_v[:, span]) + known_v[:, span].astype(f32)
        part = flipped(target_v[:, span], gate(edge_sum).astype(bf16))
        if i == 0:
            sums_v[...] = part
        else:
            sums_v[...] += part

    spare = lift_v.shape[1] - 3 * mids
    beside_first = product(beside, weights["node_w1"][...]).astype(bf16)
    lift = lift_v[...]
    if spare:
        beside = jnp.concatenate([beside, blank(spare)], axis=0)
        beside_first = jnp.concatenate([beside_first, blank(spare)], axis=0)
    lifted = (fine_v[...].astype(f32) + product(lift, beside)).astype(bf16)
    incoming = first_v[...] + product(lift, beside_first)
    incoming += product(sums_v[...].astype(bf16), ending_v[...])
    hidden = gate(incoming).astype(bf16)
    rows = fines // 2
    for half in range(2):
        span = slice(half * rows, (half + 1) * rows)
        result = lifted[span].astype(f32) + normed(product(hidden[span], weights["node_w3"][...]))
        fine_out_v[span] = result.astype(bf16)
        put(fine_out_v.at[span], fine_out_ref.at[span])
    for copy in outs:
        copy.wait()


def on_device(
    fine_latent,
    mid_latent,
    coarse_latent,
    fine_parent,
    mid_parent,
    halo_rows,
    edge_source,
    edge_target,
    w_child,
    mid_w1,
    mid_w2,
    mid_w3,
    w_coarse,
    coarse_w1,
    coarse_w2,
    coarse_w3,
    w_descend,
    w_fine,
    edge_w_src,
    edge_w_dst,
    edge_w2,
    node_w1,
    node_w2,
    node_w3,
):
    named = dict(
        w_child=w_child,
        mid_w1=mid_w1,
        mid_w2=mid_w2,
        mid_w3=mid_w3,
        w_coarse=w_coarse,
        coarse_w1=coarse_w1,
        coarse_w2=coarse_w2,
        coarse_w3=coarse_w3,
        w_descend=w_descend,
        w_fine=w_fine,
        edge_w_src=edge_w_src,
        edge_w_dst=edge_w_dst,
        edge_w2=edge_w2,
        node_w1=node_w1,
        node_w2=node_w2,
        node_w3=node_w3,
    )
    groups, tiles = (lax.axis_size("rhombus"), lax.axis_size("tile"))
    devices = groups * tiles
    fines, features = fine_latent.shape
    mids = mid_latent.shape[0]
    halos = halo_rows.shape[0]
    rims = halos // 2
    edges = edge_source.shape[0]
    coarse_count = coarse_latent.shape[0]
    width = ceil(mids)
    pairs = tiles // 2
    level = 2 if pairs == 4 else pairs - 1
    sends = groups + level + (groups - 1) * (level + 1) + groups * level
    sends += 2 * groups if pairs == 4 else 0
    vmem = pl.BlockSpec(memory_space=pltpu.VMEM)
    hbm = pl.BlockSpec(memory_space=pl.ANY)
    dma = pltpu.SemaphoreType.DMA
    square = (features, features)
    small = [fine_parent[None, :], halo_rows[None, :], mid_parent[None, :], mid_latent]
    small += [edge_source[None, :], edge_target[None, :]]
    weights = [named[name] for name in GATHER_WEIGHTS + FINISH_WEIGHTS]
    handed = (
        pltpu.VMEM((coarse_count, features), f32),
        pltpu.VMEM((features, edges), bf16),
        pltpu.VMEM((8 * mids, edges), bf16),
        pltpu.VMEM((fines, edges), bf16),
        pltpu.VMEM((fines, features), f32),
        pltpu.VMEM((fines, features), bf16),
        pltpu.VMEM((coarse_count, features), bf16),
        pltpu.VMEM((5 * mids, features), bf16),
        pltpu.VMEM((5 * mids, ceil(coarse_count)), bf16),
        pltpu.VMEM((fines, ceil(3 * mids)), bf16),
        pltpu.VMEM((2, *square), bf16),
        pltpu.VMEM(square, bf16),
        pltpu.VMEM((len(FINISH_WEIGHTS), *square), bf16),
    )
    between = pl.pallas_call(
        lambda *refs: gather_kernel(groups, tiles, *refs),
        out_shape=handed,
        in_specs=[hbm] * (len(small) + 2 + len(weights)),
        out_specs=(vmem,) * len(handed),
        scratch_shapes=[
            pltpu.VMEM((devices, mids, features), bf16),
            pltpu.VMEM((devices, 1, width), i32),
            pltpu.VMEM((halos, features), bf16),
            pltpu.VMEM((2, 1, rims), i32),
            pltpu.VMEM((len(GATHER_WEIGHTS), *square), bf16),
            *[pltpu.VMEM(array.shape, array.dtype) for array in small],
            pltpu.VMEM((2, mids, features), bf16),
            pltpu.VMEM((2, mids, features), bf16),
            pltpu.VMEM((halos, features), bf16),
            pltpu.VMEM((2, 1, rims), i32),
            pltpu.VMEM((features + 16, 2 * fines + halos), bf16),
            dma((len(small) + 2 + len(weights),)),
            dma((6,)),
            dma((6,)),
            dma((2, sends)),
            dma((devices,)),
            dma((devices,)),
        ],
        compiler_params=pltpu.CompilerParams(collective_id=0, has_side_effects=True, vmem_limit_bytes=40 << 20),
        name="sweep_gather",
    )(*small, fine_latent, coarse_latent, *weights)
    return pl.pallas_call(
        finish_kernel,
        out_shape=(
            jax.ShapeDtypeStruct((fines, features), bf16),
            jax.ShapeDtypeStruct((mids, features), bf16),
            jax.ShapeDtypeStruct((coarse_count, features), bf16),
        ),
        in_specs=[vmem] * len(handed),
        out_specs=(hbm,) * 3,
        scratch_shapes=[
            pltpu.VMEM((fines, features), bf16),
            pltpu.VMEM((mids, features), bf16),
            pltpu.VMEM((coarse_count, features), bf16),
            pltpu.VMEM((ceil(coarse_count), features), bf16),
            pltpu.VMEM((fines, features), f32),
            dma((4,)),
        ],
        compiler_params=pltpu.CompilerParams(vmem_limit_bytes=24 << 20),
        name="sweep_finish",
    )(*between)


def solution(mesh):
    split, rows, whole = (P(("rhombus", "tile")), P(("rhombus", "tile"), None), P())
    placed = (rows, rows, whole) + (split,) * 5 + (whole,) * 16
    return jax.shard_map(
        on_device,
        mesh=mesh,
        in_specs=placed,
        out_specs=(rows, rows, whole),
        check_vma=False,
    )
```

```python
import jax
import jax.numpy as jnp
from jax import lax
from jax.experimental import pallas as pl
from jax.experimental.pallas import tpu as pltpu
from jax.sharding import PartitionSpec as P

MESH = pl.DeviceIdType.MESH

EPSILON = 1e-05

bf16, f32, i32 = (jnp.bfloat16, jnp.float32, jnp.int32)

ACROSS = (((1,), (1,)), ((), ()))


def product(left, right):
    return jnp.dot(left, right, preferred_element_type=f32)


def flipped(left, right):
    return lax.dot_general(left, right, ACROSS, preferred_element_type=f32)


def normed(values):
    return values / jnp.sqrt(jnp.mean(values * values, axis=-1, keepdims=True) + EPSILON)


def gate(values):
    return values * (0.5 + 0.5 * jnp.tanh(0.5 * values))


def one_hot(ids, axis, shape):
    return jnp.where(lax.broadcasted_iota(i32, shape, axis) == ids, 1.0, 0.0).astype(bf16)


def as_columns(row, width):
    count = row.shape[1]
    column = jnp.transpose(jnp.broadcast_to(row, (128, count)))
    return jnp.concatenate([column] * (width // 128), axis=1)


def ceil(n, unit=128):
    return -(-n // unit) * unit


GATHER_WEIGHTS = (
    "w_child",
    "mid_w2",
    "mid_w1",
    "mid_w3",
    "edge_w_dst",
    "edge_w_src",
    "w_coarse",
    "coarse_w2",
    "coarse_w1",
    "edge_w2",
    "node_w2",
)
FINISH_WEIGHTS = ("node_w1", "coarse_w3", "w_descend", "w_fine", "node_w3")
SMALL = ("parent", "halo", "coarse_id", "latent")
LOADS = (2, 2, 1, 1, 2, 1, 2)


def gather_kernel(groups, tiles, *refs):
    refs = iter(refs)

    def take(n):
        return [next(refs) for _ in range(n)]

    small_refs = dict(zip(SMALL + ("source", "target"), take(len(SMALL) + 2)))
    fine_ref, coarse_ref = take(2)
    weight_refs = dict(zip(GATHER_WEIGHTS + FINISH_WEIGHTS, take(len(GATHER_WEIGHTS + FINISH_WEIGHTS))))
    pre_v, known_v, lookup_v, target_v, first_v, fine_v, coarse_v = take(7)
    near_v, pick_v, lift_v, flip_v, ending_v, handed_v = take(6)
    ups_ref, ids_ref, rim_ref, rim_parent_ref, weights_v = take(5)
    small_v = dict(zip(SMALL, take(len(SMALL))))
    (edge_ids_v,) = take(1)
    side_v, beside_v, picked_v, picked_parent_v, table_v, message_v, gained_v = take(7)
    load_sem, near_send, near_recv, tree_send, block_recv, id_send, id_recv = take(7)

    group, tile = (lax.axis_index("rhombus"), lax.axis_index("tile"))
    pairs = tiles // 2
    pair, core = (tile // 2, tile % 2)
    mids = small_v["latent"].shape[0]
    rims = small_v["halo"].shape[1] // 2
    fines, features = fine_v.shape
    coarse_count = coarse_v.shape[0]
    edges = edge_ids_v.shape[2]

    def at(group_id, pair_id, core_id):
        return (group_id, pair_id * 2 + core_id)

    if groups == 4:
        heights = [group, group + 1 - 2 * (group % 2), (group + 2) % 4, 3 - group]
    else:
        heights = [(group + k) % groups for k in [0] + sorted(range(1, groups), key=lambda k: min(k, groups - k))]
    columns = [at(height, pair, core) for height in heights[1:]]
    if pairs == 4:
        level = [pair + 1 - 2 * (pair % 2), (pair + 2) % 4]
        corner = (level[0] + 2) % 4
    else:
        level = [(pair + k) % pairs for k in range(1, pairs)]
    row_peers = [at(group, other, core) for other in level]
    partner = at(group, pair, 1 - core)
    peers = columns + row_peers + [partner]

    barrier = pltpu.get_barrier_semaphore()
    for peer in peers:
        pl.semaphore_signal(barrier, inc=1, device_id=peer, device_id_type=MESH)

    @pl.when(tile > 0)
    def _():
        pl.semaphore_signal(barrier, inc=1, device_id=(group, tile - 1), device_id_type=MESH)

    @pl.when(tile < tiles - 1)
    def _():
        pl.semaphore_signal(barrier, inc=1, device_id=(group, tile + 1), device_id_type=MESH)

    loads = {}

    def load(name, *pairs_of_refs, whole=None):
        sem = load_sem.at[len(loads)]
        for source, held in pairs_of_refs:
            pltpu.make_async_copy(source, held, sem).start()
        held = pairs_of_refs[0][1] if whole is None else whole
        loads[name] = pltpu.make_async_copy(held, held, sem)

    load("parent", (small_refs["parent"], small_v["parent"]))
    load("fine", (fine_ref, fine_v))
    for name in ("halo", "latent", "coarse_id"):
        load(name, (small_refs[name], small_v[name]))
    held = {name: weights_v.at[i] for i, name in enumerate(GATHER_WEIGHTS)}
    held.update({name: handed_v.at[i] for i, name in enumerate(FINISH_WEIGHTS)})
    first = 0
    for n, count in enumerate(LOADS):
        names = GATHER_WEIGHTS[first : first + count]
        load(n, *[(weight_refs[name], held[name]) for name in names], whole=weights_v.at[pl.ds(first, count)])
        first += count
        if n == 1:
            ids = [(small_refs[name], edge_ids_v.at[i]) for i, name in enumerate(("source", "target"))]
            load("edges", *ids, whole=edge_ids_v)
        if n == 4:
            load("coarse", (coarse_ref, coarse_v))
    load("node_w1", (weight_refs["node_w1"], held["node_w1"]))
    rest = FINISH_WEIGHTS[1:]
    load("handed", *[(weight_refs[name], held[name]) for name in rest], whole=handed_v.at[pl.ds(1, len(rest))])
    waited = set()

    def await_load(name):
        if name not in waited:
            loads[name].wait()
            waited.add(name)

    def weight(name):
        if name == "node_w1":
            await_load(name)
        else:
            place = GATHER_WEIGHTS.index(name)
            await_load(next(n for n in range(len(LOADS)) if place < sum(LOADS[: n + 1])))
        return held[name][...]

    me = group * tiles + tile
    halves = groups * pairs

    def place_of(group_id, pair_id, core_id):
        return core_id * halves + pair_id * groups + group_id

    mine = place_of(group, pair, core)
    await_load("parent")
    parents = small_v["parent"][...]
    picker = one_hot(parents, 0, (3 * mids, fines))
    await_load("fine")
    sums = product(picker, fine_v[...])
    side_v[0] = sums[mids : 2 * mids].astype(bf16)
    side_v[1] = sums[2 * mids :].astype(bf16)
    pl.semaphore_wait(barrier, len(peers) + 1 + (tile + tiles - 1) // tiles - (tile + 1) // tiles)

    def near(index, source, target, device):
        return pltpu.make_async_remote_copy(
            src_ref=source,
            dst_ref=target,
            send_sem=near_send.at[index],
            recv_sem=near_recv.at[index],
            device_id=device,
            device_id_type=MESH,
        )

    before, after = ((group, tile - 1), (group, tile + 1))
    to_before = [
        near(0, side_v.at[0], beside_v.at[0], before),
        near(1, picked_v.at[pl.ds(0, rims)], rim_ref.at[pl.ds(rims, rims)], before),
        near(2, picked_parent_v.at[0], rim_parent_ref.at[1], before),
    ]
    to_after = [
        near(3, side_v.at[1], beside_v.at[1], after),
        near(4, picked_v.at[pl.ds(rims, rims)], rim_ref.at[pl.ds(0, rims)], after),
        near(5, picked_parent_v.at[1], rim_parent_ref.at[0], after),
    ]

    @pl.when(tile > 0)
    def _():
        to_before[0].start()

    @pl.when(tile < tiles - 1)
    def _():
        to_after[0].start()

    ids_sent = []

    def pass_ids(first_slot, count, device, kind):
        copy = pltpu.make_async_remote_copy(
            src_ref=ids_ref.at[pl.ds(first_slot, count)],
            dst_ref=ids_ref.at[pl.ds(first_slot, count)],
            send_sem=id_send.at[0],
            recv_sem=id_recv.at[kind],
            device_id=device,
            device_id_type=MESH,
        )
        copy.start()
        ids_sent.append(count)

    def await_ids(first_slot, count, kind):
        held_ids = ids_ref.at[pl.ds(first_slot, count)]
        pltpu.make_async_copy(held_ids, held_ids, id_recv.at[kind]).wait()

    def column_of(pair_id, core_id):
        return place_of(0, pair_id, core_id)

    await_load("coarse_id")
    spare_ids = jnp.zeros((1, ids_ref.shape[2] - mids), i32)
    ids_ref[mine] = jnp.concatenate([small_v["coarse_id"][...], spare_ids], axis=1)
    for device in columns:
        pass_ids(mine, 1, device, 0)

    def ids_across():
        await_ids(0, groups - 1, 0)
        for n, device in enumerate(row_peers):
            pass_ids(column_of(pair, core), groups, device, 1 + n)

    def ids_corner():
        for n, other in enumerate(level):
            await_ids(column_of(other, core), groups, 1 + n if pairs == 4 else len(level) - n)
        if pairs == 4:
            pass_ids(column_of(level[0], core), groups, row_peers[1], len(level) + 1)

    def ids_partner():
        if pairs == 4:
            await_ids(column_of(corner, core), groups, len(level) + 1)
        pass_ids(core * halves, halves, partner, len(level) + 2)

    def ids_done():
        await_ids((1 - core) * halves, halves, len(level) + 2)

    await_load("halo")
    halo = small_v["halo"][...]
    picked_v[...] = product(one_hot(as_columns(halo, fines), 1, (2 * rims, fines)), fine_v[...]).astype(bf16)
    side = parents // mids
    shift = jnp.where(side == 1, -1, jnp.where(side == 2, 1, 0))
    within = parents % mids
    parent_column = jnp.transpose(jnp.broadcast_to((me + shift) * mids + within, (128, fines)))
    for half in range(2):
        hit = lax.broadcasted_iota(i32, (fines, rims), 0) == halo[:, half * rims : (half + 1) * rims]
        spread = jnp.concatenate([parent_column] * (rims // 128), axis=1)
        picked_parent_v[half] = jnp.sum(jnp.where(hit, spread, 0), axis=0, keepdims=True)

    @pl.when(tile > 0)
    def _():
        to_before[1].start()
        to_before[2].start()

    @pl.when(tile < tiles - 1)
    def _():
        to_after[1].start()
        to_after[2].start()

    child_mid = product(weight("w_child"), weight("mid_w2")).astype(bf16)
    await_load("latent")
    kept_mid = product(small_v["latent"][...], weight("mid_w1"))
    flip_v[1] = jnp.transpose(weight("edge_w_dst"))
    table_v[:features, fines + 2 * rims :] = flipped(flip_v[1], fine_v[...]).astype(bf16)
    flip_v[0] = jnp.transpose(weight("edge_w_src"))
    table_v[:features, :fines] = flipped(flip_v[0], fine_v[...]).astype(bf16)
    mid_w3 = weight("mid_w3")

    @pl.when(tile > 0)
    def _():
        to_after[0].wait_recv()

    @pl.when(tile == 0)
    def _():
        beside_v[1] = jnp.zeros_like(beside_v[1])
        rim_ref[pl.ds(0, rims)] = jnp.zeros((rims, features), bf16)
        rim_parent_ref[0] = jnp.full(rim_parent_ref.shape[1:], -1, i32)

    @pl.when(tile < tiles - 1)
    def _():
        to_before[0].wait_recv()

    @pl.when(tile == tiles - 1)
    def _():
        beside_v[0] = jnp.zeros_like(beside_v[0])
        rim_ref[pl.ds(rims, rims)] = jnp.zeros((rims, features), bf16)
        rim_parent_ref[1] = jnp.full(rim_parent_ref.shape[1:], -1, i32)

    total = (sums[:mids] + beside_v[0].astype(f32) + beside_v[1].astype(f32)).astype(bf16)
    hidden = gate(kept_mid + product(total, child_mid)).astype(bf16)
    mid_up = small_v["latent"][...].astype(f32) + normed(product(hidden, mid_w3))
    ups_ref[mine] = mid_up.astype(bf16)

    started = []
    sides = {"column": 0, "near": 1, "far": 2, "corner": 3}

    def block_copy(slot, recv, device):
        return pltpu.make_async_remote_copy(
            src_ref=ups_ref.at[slot],
            dst_ref=ups_ref.at[slot],
            send_sem=tree_send.at[0],
            recv_sem=block_recv.at[recv],
            device_id=device,
            device_id_type=MESH,
        )

    def send(pair_id, height, devices, side):
        slot = place_of(height, pair_id, core)
        for device in devices:
            own_way = device is not partner
            copy = block_copy(slot, slot - core * halves if own_way else halves + side, device)
            copy.start()
            started.append(copy)

    def arrive(pair_id, height):
        slot = place_of(height, pair_id, core)
        block_copy(slot, slot - core * halves, partner).wait_recv()

    def arrive_column(pair_id, side):
        held_blocks = ups_ref.at[pl.ds(column_of(pair_id, 1 - core), groups)]
        pltpu.make_async_copy(held_blocks, held_blocks, block_recv.at[halves + side]).wait()

    send(pair, group, columns[:1] + row_peers + columns[1:] + [partner], 0)

    def keep_coarse():
        await_load("coarse")
        pre_v[...] = product(coarse_v[...], weight("coarse_w1"))

    def keep_message():
        message_v[...] = product(weight("w_coarse"), weight("coarse_w2")).astype(bf16)

    def keep_ending():
        ending_v[...] = product(weight("edge_w2"), weight("node_w2")).astype(bf16)

    def keep_first():
        first_v[...] = product(fine_v[...], weight("node_w1"))

    own_near = (1 + shift) * mids + within

    def fill_table():
        @pl.when(tile > 0)
        def _():
            for copy in to_after[1:]:
                copy.wait_recv()

        @pl.when(tile < tiles - 1)
        def _():
            for copy in to_before[1:]:
                copy.wait_recv()

        table_v[:features, fines : fines + 2 * rims] = flipped(flip_v[0], rim_ref[...]).astype(bf16)
        far = jnp.concatenate([rim_parent_ref[0], rim_parent_ref[1]], axis=1)
        far = jnp.where(far < 0, -1, far - (me - 2) * mids)
        blank = jnp.zeros((1, fines), i32)
        source_parent = jnp.concatenate([own_near + mids, far, blank], axis=1)
        target_parent = jnp.concatenate([blank, jnp.zeros((1, 2 * rims), i32), own_near], axis=1)
        line = lax.broadcasted_iota(i32, (table_v.shape[0] - features, table_v.shape[1]), 0)
        named = jnp.where(line == 0, source_parent, jnp.where(line == 1, target_parent, 0))
        table_v[features:] = named.astype(f32).astype(bf16)
        lift_v[...] = one_hot(as_columns(own_near, lift_v.shape[1]), 1, lift_v.shape)

    step = next(size for size in (512, 256, 128) if edges % size == 0)

    def known(i):
        span = pl.ds(i * step, step)
        source_pick = one_hot(edge_ids_v[0, :, span], 0, (fines + 2 * rims, step))
        target_pick = one_hot(edge_ids_v[1, :, span], 0, (fines, step))
        target_v[:, span] = target_pick
        found = product(table_v[...], jnp.concatenate([source_pick, target_pick], axis=0))
        known_v[:, span] = found[:features].astype(bf16)
        source_near = found[features : features + 1].astype(i32)
        target_near = found[features + 1 : features + 2].astype(i32) + 5 * mids
        line = lax.broadcasted_iota(i32, (8 * mids, step), 0)
        lookup_v[:, span] = jnp.where((line == source_near) | (line == target_near), 1.0, 0.0).astype(bf16)

    blocks_of_edges = iter(range(edges // step))

    def do_known(n=1):
        await_load("edges")
        for i in [i for _, i in zip(range(n), blocks_of_edges)]:
            known(i)

    def coarse_part(places, rows_of):
        blocks = jnp.concatenate([rows_of(place) for place in places], axis=0)
        slots = [place + h for place in places for h in range(groups)]
        id_row = jnp.concatenate([ids_ref[slot][:, :mids] for slot in slots], axis=1)
        return product(one_hot(id_row, 0, (coarse_count, len(slots) * mids)), blocks)

    nearby = []
    for d in range(-2, 3):
        other = (me + d + 2 * groups * tiles) % (groups * tiles)
        other_tile = other % tiles
        nearby.append(place_of(other // tiles, other_tile // 2, other_tile % 2))

    def find_near():
        window, padded = pick_v.shape
        spare = ceil(window) - window
        near_row = jnp.concatenate([ids_ref[slot][:, :mids] for slot in nearby] + [jnp.zeros((1, spare), i32)], axis=1)
        pick_v[...] = one_hot(as_columns(near_row, padded)[:window], 1, (window, padded))

    def column_rows(place):
        return ups_ref[pl.ds(place, groups)].reshape(groups * mids, features)

    ids_across()
    fill_table()
    do_known()
    if pairs == 4:
        near_pair, far_pair = level

        def across_at(n):
            arrive(near_pair, heights[n])
            send(near_pair, heights[n], ([row_peers[1]] if n % 2 == 0 else []) + [partner], 1)
            arrive(far_pair, heights[n])
            send(far_pair, heights[n], ([row_peers[0]] if n % 2 == 1 else []) + [partner], 2)

        def corner_at(n):
            arrive(corner, heights[n])
            send(corner, heights[n], [partner], 3)

        def column_at(n):
            arrive(pair, heights[n])
            send(pair, heights[n], row_peers + [partner], 0)

        keep_message()
        column_at(1)
        across_at(0)
        do_known()
        ids_corner()
        column_at(2)
        keep_coarse()
        column_at(3)
        do_known()
        across_at(1)
        do_known()
        ids_partner()
        corner_at(0)
        across_at(2)
        keep_ending()
        keep_first()
        across_at(3)
        corner_at(1)
        do_known()
        corner_at(2)
        do_known(edges)
        corner_at(3)
        ids_done()
        find_near()
        mine_first = [column_of(p, core) for p in (pair, near_pair, far_pair, corner)]
        arrive_column(pair, 0)
        arrive_column(near_pair, 1)
        arrive_column(far_pair, 2)
        other_first = [column_of(p, 1 - core) for p in (pair, near_pair, far_pair)]
        gained_v[...] = coarse_part(mine_first + other_first, column_rows)
        arrive_column(corner, 3)
        gained_v[...] += coarse_part([column_of(corner, 1 - core)], column_rows)
    else:
        for height in heights[1:]:
            arrive(pair, height)
            send(pair, height, row_peers + [partner], 0)
        for height in heights:
            for n, other in enumerate(level):
                arrive(other, height)
                send(other, height, [partner], 1 + n)
        for keep in (keep_message, keep_coarse, keep_ending, keep_first):
            keep()
        do_known(edges)
        ids_corner()
        ids_partner()
        ids_done()
        for n, other in enumerate([pair] + level):
            arrive_column(other, n)

        find_near()
        gained_v[...] = jnp.zeros_like(gained_v)

        def part(i, carry):
            gained_v[...] += coarse_part([i * groups], column_rows)
            return carry

        lax.fori_loop(0, 2 * pairs, part, 0)

    pre_v[...] += product(gained_v[...].astype(bf16), message_v[...])
    near_v[...] = jnp.concatenate([ups_ref[slot] for slot in nearby], axis=0)

    @pl.when(tile > 0)
    def _():
        for copy in to_before:
            copy.wait_send()

    @pl.when(tile < tiles - 1)
    def _():
        for copy in to_after:
            copy.wait_send()

    total = sum(ids_sent)
    for first in range(0, total, ids_ref.shape[0]):
        sent = ids_ref.at[pl.ds(0, min(total - first, ids_ref.shape[0]))]
        pltpu.make_async_copy(sent, sent, id_send.at[0]).wait()
    for first in range(0, len(started), ups_ref.shape[0]):
        blocks = ups_ref.at[pl.ds(0, min(len(started) - first, ups_ref.shape[0]))]
        pltpu.make_async_copy(blocks, blocks, tree_send.at[0]).wait()
    await_load("handed")


def finish_kernel(*refs):
    pre_v, known_v, lookup_v, target_v, first_v, fine_v, coarse_v = refs[:7]
    near_v, pick_v, lift_v, flip_v, ending_v, handed_v = refs[7:13]
    fine_out_ref, mid_out_ref, coarse_out_ref = refs[13:16]
    fine_out_v, mid_out_v, coarse_out_v, padded_v, sums_v, out_sem = refs[16:]
    window, padded = pick_v.shape
    mids = mid_out_v.shape[0]
    fines, features = fine_v.shape
    coarse_count = coarse_v.shape[0]
    edges = known_v.shape[1]
    weights = {name: handed_v.at[i] for i, name in enumerate(FINISH_WEIGHTS)}
    outs = []

    def put(source, target):
        outs.append(pltpu.make_async_copy(source, target, out_sem.at[len(outs)]))
        outs[-1].start()

    hidden = gate(pre_v[...]).astype(bf16)
    updated = (coarse_v[...].astype(f32) + normed(product(hidden, weights["coarse_w3"][...]))).astype(bf16)
    coarse_out_v[...] = updated
    put(coarse_out_v, coarse_out_ref)
    edge = coarse_count // 16 * 16
    padded_v[edge:] = jnp.zeros((padded - edge, features), bf16)
    padded_v[:coarse_count] = updated

    picked = product(pick_v[...], padded_v[...]).astype(bf16)
    down = product(picked, weights["w_descend"][...])
    near_out = (near_v[...].astype(f32) + down).astype(bf16)
    mid_out_v[...] = near_out[2 * mids : 3 * mids]
    put(mid_out_v, mid_out_ref)
    fine_down = product(near_out, weights["w_fine"][...]).astype(bf16)
    beside = fine_down[mids : 4 * mids]

    def blank(rows):
        return jnp.zeros((rows, features), bf16)

    source_rows = jnp.concatenate([fine_down, blank(3 * mids)], axis=0)
    target_rows = jnp.concatenate([blank(5 * mids), beside], axis=0)
    change = (flipped(flip_v[0], source_rows) + flipped(flip_v[1], target_rows)).astype(bf16)

    step = next(size for size in (1024, 512, 256, 128) if edges % size == 0)
    total = None
    for i in range(edges // step):
        span = slice(i * step, (i + 1) * step)
        edge_sum = product(change, lookup_v[:, span]) + known_v[:, span].astype(f32)
        part = flipped(target_v[:, span], gate(edge_sum).astype(bf16))
        if i == 0:
            sums_v[...] = part
        else:
            sums_v[...] += part

    spare = lift_v.shape[1] - 3 * mids
    beside_first = product(beside, weights["node_w1"][...]).astype(bf16)
    lift = lift_v[...]
    if spare:
        beside = jnp.concatenate([beside, blank(spare)], axis=0)
        beside_first = jnp.concatenate([beside_first, blank(spare)], axis=0)
    lifted = (fine_v[...].astype(f32) + product(lift, beside)).astype(bf16)
    incoming = first_v[...] + product(lift, beside_first)
    incoming += product(sums_v[...].astype(bf16), ending_v[...])
    hidden = gate(incoming).astype(bf16)
    rows = fines // 2
    for half in range(2):
        span = slice(half * rows, (half + 1) * rows)
        result = lifted[span].astype(f32) + normed(product(hidden[span], weights["node_w3"][...]))
        fine_out_v[span] = result.astype(bf16)
        put(fine_out_v.at[span], fine_out_ref.at[span])
    for copy in outs:
        copy.wait()


def on_device(
    fine_latent,
    mid_latent,
    coarse_latent,
    fine_parent,
    mid_parent,
    halo_rows,
    edge_source,
    edge_target,
    w_child,
    mid_w1,
    mid_w2,
    mid_w3,
    w_coarse,
    coarse_w1,
    coarse_w2,
    coarse_w3,
    w_descend,
    w_fine,
    edge_w_src,
    edge_w_dst,
    edge_w2,
    node_w1,
    node_w2,
    node_w3,
):
    named = dict(
        w_child=w_child,
        mid_w1=mid_w1,
        mid_w2=mid_w2,
        mid_w3=mid_w3,
        w_coarse=w_coarse,
        coarse_w1=coarse_w1,
        coarse_w2=coarse_w2,
        coarse_w3=coarse_w3,
        w_descend=w_descend,
        w_fine=w_fine,
        edge_w_src=edge_w_src,
        edge_w_dst=edge_w_dst,
        edge_w2=edge_w2,
        node_w1=node_w1,
        node_w2=node_w2,
        node_w3=node_w3,
    )
    groups, tiles = (lax.axis_size("rhombus"), lax.axis_size("tile"))
    devices = groups * tiles
    fines, features = fine_latent.shape
    mids = mid_latent.shape[0]
    halos = halo_rows.shape[0]
    rims = halos // 2
    edges = edge_source.shape[0]
    coarse_count = coarse_latent.shape[0]
    width = ceil(mids)
    pairs = tiles // 2
    level = 2 if pairs == 4 else pairs - 1
    vmem = pl.BlockSpec(memory_space=pltpu.VMEM)
    hbm = pl.BlockSpec(memory_space=pl.ANY)
    dma = pltpu.SemaphoreType.DMA
    square = (features, features)
    small = [fine_parent[None, :], halo_rows[None, :], mid_parent[None, :], mid_latent]
    edge_ids = [edge_source[None, :], edge_target[None, :]]
    weights = [named[name] for name in GATHER_WEIGHTS + FINISH_WEIGHTS]
    handed = (
        pltpu.VMEM((coarse_count, features), f32),
        pltpu.VMEM((features, edges), bf16),
        pltpu.VMEM((8 * mids, edges), bf16),
        pltpu.VMEM((fines, edges), bf16),
        pltpu.VMEM((fines, features), f32),
        pltpu.VMEM((fines, features), bf16),
        pltpu.VMEM((coarse_count, features), bf16),
        pltpu.VMEM((5 * mids, features), bf16),
        pltpu.VMEM((5 * mids, ceil(coarse_count)), bf16),
        pltpu.VMEM((fines, ceil(3 * mids)), bf16),
        pltpu.VMEM((2, *square), bf16),
        pltpu.VMEM(square, bf16),
        pltpu.VMEM((len(FINISH_WEIGHTS), *square), bf16),
    )
    between = pl.pallas_call(
        lambda *refs: gather_kernel(groups, tiles, *refs),
        out_shape=handed,
        in_specs=[hbm] * (len(small) + 4 + len(weights)),
        out_specs=(vmem,) * len(handed),
        scratch_shapes=[
            pltpu.VMEM((devices, mids, features), bf16),
            pltpu.VMEM((devices, 1, width), i32),
            pltpu.VMEM((halos, features), bf16),
            pltpu.VMEM((2, 1, rims), i32),
            pltpu.VMEM((len(GATHER_WEIGHTS), *square), bf16),
            *[pltpu.VMEM(array.shape, array.dtype) for array in small],
            pltpu.VMEM((2, 1, edges), i32),
            pltpu.VMEM((2, mids, features), bf16),
            pltpu.VMEM((2, mids, features), bf16),
            pltpu.VMEM((halos, features), bf16),
            pltpu.VMEM((2, 1, rims), i32),
            pltpu.VMEM((features + 16, 2 * fines + halos), bf16),
            pltpu.VMEM(square, bf16),
            pltpu.VMEM((coarse_count, features), f32),
            dma((len(small) + 5 + len(LOADS),)),
            dma((6,)),
            dma((6,)),
            dma((1,)),
            dma((groups * pairs + level + 2,)),
            dma((1,)),
            dma((level + 3,)),
        ],
        compiler_params=pltpu.CompilerParams(collective_id=0, has_side_effects=True, vmem_limit_bytes=40 << 20),
        name="sweep_gather",
    )(*small, *edge_ids, fine_latent, coarse_latent, *weights)
    return pl.pallas_call(
        finish_kernel,
        out_shape=(
            jax.ShapeDtypeStruct((fines, features), bf16),
            jax.ShapeDtypeStruct((mids, features), bf16),
            jax.ShapeDtypeStruct((coarse_count, features), bf16),
        ),
        in_specs=[vmem] * len(handed),
        out_specs=(hbm,) * 3,
        scratch_shapes=[
            pltpu.VMEM((fines, features), bf16),
            pltpu.VMEM((mids, features), bf16),
            pltpu.VMEM((coarse_count, features), bf16),
            pltpu.VMEM((ceil(coarse_count), features), bf16),
            pltpu.VMEM((fines, features), f32),
            dma((4,)),
        ],
        compiler_params=pltpu.CompilerParams(vmem_limit_bytes=24 << 20),
        name="sweep_finish",
    )(*between)


def solution(mesh):
    split, rows, whole = (P(("rhombus", "tile")), P(("rhombus", "tile"), None), P())
    placed = (rows, rows, whole) + (split,) * 5 + (whole,) * 16
    return jax.shard_map(
        on_device,
        mesh=mesh,
        in_specs=placed,
        out_specs=(rows, rows, whole),
        check_vma=False,
    )
```

```python
import jax
import jax.numpy as jnp
from jax import lax
from jax.experimental import pallas as pl
from jax.experimental.pallas import tpu as pltpu
from jax.sharding import PartitionSpec as P

MESH = pl.DeviceIdType.MESH

EPSILON = 1e-05

bf16, f32, i32 = (jnp.bfloat16, jnp.float32, jnp.int32)

ACROSS = (((1,), (1,)), ((), ()))


def product(left, right):
    return jnp.dot(left, right, preferred_element_type=f32)


def flipped(left, right):
    return lax.dot_general(left, right, ACROSS, preferred_element_type=f32)


def normed(values):
    return values / jnp.sqrt(jnp.mean(values * values, axis=-1, keepdims=True) + EPSILON)


def gate(values):
    return values * (0.5 + 0.5 * jnp.tanh(0.5 * values))


def one_hot(ids, axis, shape):
    return jnp.where(lax.broadcasted_iota(i32, shape, axis) == ids, 1.0, 0.0).astype(bf16)


def as_columns(row, width):
    count = row.shape[1]
    column = jnp.transpose(jnp.broadcast_to(row, (128, count)))
    return jnp.concatenate([column] * (width // 128), axis=1)


def ceil(n, unit=128):
    return -(-n // unit) * unit


GATHER_WEIGHTS = (
    "w_child",
    "mid_w2",
    "mid_w1",
    "mid_w3",
    "edge_w_dst",
    "edge_w_src",
    "w_coarse",
    "coarse_w2",
    "coarse_w1",
    "edge_w2",
    "node_w2",
)
FINISH_WEIGHTS = ("node_w1", "coarse_w3", "w_descend", "w_fine", "node_w3")
SMALL = ("parent", "halo", "coarse_id", "latent")
LOADS = (2, 2, 1, 1, 2, 1, 2)


def gather_kernel(groups, tiles, *refs):
    refs = iter(refs)

    def take(n):
        return [next(refs) for _ in range(n)]

    small_refs = dict(zip(SMALL + ("source", "target"), take(len(SMALL) + 2)))
    fine_ref, coarse_ref = take(2)
    weight_refs = dict(zip(GATHER_WEIGHTS + FINISH_WEIGHTS, take(len(GATHER_WEIGHTS + FINISH_WEIGHTS))))
    pre_v, known_v, lookup_v, target_v, first_v, fine_v, coarse_v = take(7)
    near_v, pick_v, lift_v, flip_v, ending_v, handed_v, message_v, gained_v = take(8)
    ups_ref, ids_ref, rim_ref, rim_parent_ref, weights_v = take(5)
    small_v = dict(zip(SMALL, take(len(SMALL))))
    (edge_ids_v,) = take(1)
    side_v, beside_v, picked_v, picked_parent_v, table_v = take(5)
    load_sem, near_send, near_recv, tree_send, block_recv, id_send, id_recv = take(7)

    group, tile = (lax.axis_index("rhombus"), lax.axis_index("tile"))
    pairs = tiles // 2
    pair, core = (tile // 2, tile % 2)
    mids = small_v["latent"].shape[0]
    rims = small_v["halo"].shape[1] // 2
    fines, features = fine_v.shape
    coarse_count = coarse_v.shape[0]
    edges = edge_ids_v.shape[2]

    def at(group_id, pair_id, core_id):
        return (group_id, pair_id * 2 + core_id)

    if groups == 4:
        heights = [group, group + 1 - 2 * (group % 2), (group + 2) % 4, 3 - group]
    else:
        order = [0] + sorted(range(1, groups), key=lambda k: min(k, groups - k))
        heights = [(group + k) % groups for k in order]
    columns = [at(height, pair, core) for height in heights[1:]]
    if pairs == 4:
        beside = pair + 1 - 2 * (pair % 2)
        level = [beside, (pair + 2) % 4, (beside + 2) % 4]
    else:
        level = [(pair + k) % pairs for k in range(1, pairs)]
    row_peers = [at(group, other, core) for other in level]
    partner = at(group, pair, 1 - core)
    peers = columns + row_peers + [partner]

    barrier = pltpu.get_barrier_semaphore()
    for peer in peers:
        pl.semaphore_signal(barrier, inc=1, device_id=peer, device_id_type=MESH)

    @pl.when(tile > 0)
    def _():
        pl.semaphore_signal(barrier, inc=1, device_id=(group, tile - 1), device_id_type=MESH)

    @pl.when(tile < tiles - 1)
    def _():
        pl.semaphore_signal(barrier, inc=1, device_id=(group, tile + 1), device_id_type=MESH)

    loads = {}

    def load(name, *pairs_of_refs, whole=None):
        sem = load_sem.at[len(loads)]
        for source, held in pairs_of_refs:
            pltpu.make_async_copy(source, held, sem).start()
        held = pairs_of_refs[0][1] if whole is None else whole
        loads[name] = pltpu.make_async_copy(held, held, sem)

    load("parent", (small_refs["parent"], small_v["parent"]))
    load("fine", (fine_ref, fine_v))
    for name in ("halo", "latent", "coarse_id"):
        load(name, (small_refs[name], small_v[name]))
    held = {name: weights_v.at[i] for i, name in enumerate(GATHER_WEIGHTS)}
    held.update({name: handed_v.at[i] for i, name in enumerate(FINISH_WEIGHTS)})
    first = 0
    for n, count in enumerate(LOADS):
        names = GATHER_WEIGHTS[first : first + count]
        load(n, *[(weight_refs[name], held[name]) for name in names], whole=weights_v.at[pl.ds(first, count)])
        first += count
        if n == 1:
            ids = [(small_refs[name], edge_ids_v.at[i]) for i, name in enumerate(("source", "target"))]
            load("edges", *ids, whole=edge_ids_v)
        if n == 4:
            load("coarse", (coarse_ref, coarse_v))
    load("node_w1", (weight_refs["node_w1"], held["node_w1"]))
    rest = FINISH_WEIGHTS[1:]
    load("handed", *[(weight_refs[name], held[name]) for name in rest], whole=handed_v.at[pl.ds(1, len(rest))])
    waited = set()

    def await_load(name):
        if name not in waited:
            loads[name].wait()
            waited.add(name)

    def weight(name):
        if name == "node_w1":
            await_load(name)
        else:
            place = GATHER_WEIGHTS.index(name)
            await_load(next(n for n in range(len(LOADS)) if place < sum(LOADS[: n + 1])))
        return held[name][...]

    me = group * tiles + tile
    halves = groups * pairs

    def place_of(group_id, pair_id, core_id):
        return core_id * halves + group_id * pairs + pair_id

    def id_place_of(group_id, pair_id, core_id):
        return core_id * halves + pair_id * groups + group_id

    mine = place_of(group, pair, core)
    await_load("parent")
    parents = small_v["parent"][...]
    picker = one_hot(parents, 0, (3 * mids, fines))
    await_load("fine")
    sums = product(picker, fine_v[...])
    side_v[0] = sums[mids : 2 * mids].astype(bf16)
    side_v[1] = sums[2 * mids :].astype(bf16)
    pl.semaphore_wait(barrier, len(peers) + 1 + (tile + tiles - 1) // tiles - (tile + 1) // tiles)

    def near(index, source, target, device):
        return pltpu.make_async_remote_copy(
            src_ref=source,
            dst_ref=target,
            send_sem=near_send.at[index],
            recv_sem=near_recv.at[index],
            device_id=device,
            device_id_type=MESH,
        )

    before, after = ((group, tile - 1), (group, tile + 1))
    to_before = [
        near(0, side_v.at[0], beside_v.at[0], before),
        near(1, picked_v.at[pl.ds(0, rims)], rim_ref.at[pl.ds(rims, rims)], before),
        near(2, picked_parent_v.at[0], rim_parent_ref.at[1], before),
    ]
    to_after = [
        near(3, side_v.at[1], beside_v.at[1], after),
        near(4, picked_v.at[pl.ds(rims, rims)], rim_ref.at[pl.ds(0, rims)], after),
        near(5, picked_parent_v.at[1], rim_parent_ref.at[0], after),
    ]

    @pl.when(tile > 0)
    def _():
        to_before[0].start()

    @pl.when(tile < tiles - 1)
    def _():
        to_after[0].start()

    ids_sent = []

    def pass_ids(first_slot, count, device, kind):
        copy = pltpu.make_async_remote_copy(
            src_ref=ids_ref.at[pl.ds(first_slot, count)],
            dst_ref=ids_ref.at[pl.ds(first_slot, count)],
            send_sem=id_send.at[0],
            recv_sem=id_recv.at[kind],
            device_id=device,
            device_id_type=MESH,
        )
        copy.start()
        ids_sent.append(count)

    def await_ids(first_slot, count, kind):
        held_ids = ids_ref.at[pl.ds(first_slot, count)]
        pltpu.make_async_copy(held_ids, held_ids, id_recv.at[kind]).wait()

    def column_of(pair_id, core_id):
        return id_place_of(0, pair_id, core_id)

    await_load("coarse_id")
    spare_ids = jnp.zeros((1, ids_ref.shape[2] - mids), i32)
    my_id = id_place_of(group, pair, core)
    ids_ref[my_id] = jnp.concatenate([small_v["coarse_id"][...], spare_ids], axis=1)
    for device in columns:
        pass_ids(my_id, 1, device, 0)

    def ids_across():
        await_ids(0, groups - 1, 0)
        for n, device in enumerate(row_peers):
            pass_ids(column_of(pair, core), groups, device, 1 + n)

    def ids_partner():
        for n, other in enumerate(level):
            await_ids(column_of(other, core), groups, 1 + n if pairs == 4 else len(level) - n)
        pass_ids(core * halves, halves, partner, len(level) + 1)

    def ids_done():
        await_ids((1 - core) * halves, halves, len(level) + 1)

    await_load("halo")
    halo = small_v["halo"][...]
    picked_v[...] = product(one_hot(as_columns(halo, fines), 1, (2 * rims, fines)), fine_v[...]).astype(bf16)
    side = parents // mids
    shift = jnp.where(side == 1, -1, jnp.where(side == 2, 1, 0))
    within = parents % mids
    parent_column = jnp.transpose(jnp.broadcast_to((me + shift) * mids + within, (128, fines)))
    for half in range(2):
        hit = lax.broadcasted_iota(i32, (fines, rims), 0) == halo[:, half * rims : (half + 1) * rims]
        spread = jnp.concatenate([parent_column] * (rims // 128), axis=1)
        picked_parent_v[half] = jnp.sum(jnp.where(hit, spread, 0), axis=0, keepdims=True)

    @pl.when(tile > 0)
    def _():
        to_before[1].start()
        to_before[2].start()

    @pl.when(tile < tiles - 1)
    def _():
        to_after[1].start()
        to_after[2].start()

    child_mid = product(weight("w_child"), weight("mid_w2")).astype(bf16)
    await_load("latent")
    kept_mid = product(small_v["latent"][...], weight("mid_w1"))
    flip_v[1] = jnp.transpose(weight("edge_w_dst"))
    table_v[:features, fines + 2 * rims :] = flipped(flip_v[1], fine_v[...]).astype(bf16)
    flip_v[0] = jnp.transpose(weight("edge_w_src"))
    table_v[:features, :fines] = flipped(flip_v[0], fine_v[...]).astype(bf16)
    mid_w3 = weight("mid_w3")

    @pl.when(tile > 0)
    def _():
        to_after[0].wait_recv()

    @pl.when(tile == 0)
    def _():
        beside_v[1] = jnp.zeros_like(beside_v[1])
        rim_ref[pl.ds(0, rims)] = jnp.zeros((rims, features), bf16)
        rim_parent_ref[0] = jnp.full(rim_parent_ref.shape[1:], -1, i32)

    @pl.when(tile < tiles - 1)
    def _():
        to_before[0].wait_recv()

    @pl.when(tile == tiles - 1)
    def _():
        beside_v[0] = jnp.zeros_like(beside_v[0])
        rim_ref[pl.ds(rims, rims)] = jnp.zeros((rims, features), bf16)
        rim_parent_ref[1] = jnp.full(rim_parent_ref.shape[1:], -1, i32)

    total = (sums[:mids] + beside_v[0].astype(f32) + beside_v[1].astype(f32)).astype(bf16)
    hidden = gate(kept_mid + product(total, child_mid)).astype(bf16)
    mid_up = small_v["latent"][...].astype(f32) + normed(product(hidden, mid_w3))
    ups_ref[mine] = mid_up.astype(bf16)

    started = []

    def send(pair_id, n, devices, recv):
        slot = place_of(heights[n], pair_id, core)
        for device in devices:
            copy = pltpu.make_async_remote_copy(
                src_ref=ups_ref.at[slot],
                dst_ref=ups_ref.at[slot],
                send_sem=tree_send.at[0],
                recv_sem=block_recv.at[recv],
                device_id=device,
                device_id_type=MESH,
            )
            copy.start()
            started.append(copy)

    def arrive(first_slot, count, recv):
        blocks = ups_ref.at[pl.ds(first_slot, count)]
        pltpu.make_async_copy(blocks, blocks, block_recv.at[recv]).wait()

    def place_in(n):
        return n if groups == 4 else order.index((groups - order[n]) % groups)

    def spread(n):
        send(pair, n, row_peers, groups + n)
        send(pair, n, [partner], 2 * groups + n)

    for n in range(1, groups):
        send(pair, 0, [columns[n - 1]], place_in(n))
        if n == 1:
            spread(0)


    def keep_coarse():
        await_load("coarse")
        pre_v[...] = product(coarse_v[...], weight("coarse_w1"))

    def keep_message():
        message_v[...] = product(weight("w_coarse"), weight("coarse_w2")).astype(bf16)

    def keep_ending():
        ending_v[...] = product(weight("edge_w2"), weight("node_w2")).astype(bf16)

    def keep_first():
        first_v[...] = product(fine_v[...], weight("node_w1"))

    own_near = (1 + shift) * mids + within

    def fill_table():
        @pl.when(tile > 0)
        def _():
            for copy in to_after[1:]:
                copy.wait_recv()

        @pl.when(tile < tiles - 1)
        def _():
            for copy in to_before[1:]:
                copy.wait_recv()

        table_v[:features, fines : fines + 2 * rims] = flipped(flip_v[0], rim_ref[...]).astype(bf16)
        far = jnp.concatenate([rim_parent_ref[0], rim_parent_ref[1]], axis=1)
        far = jnp.where(far < 0, -1, far - (me - 2) * mids)
        blank = jnp.zeros((1, fines), i32)
        source_parent = jnp.concatenate([own_near + mids, far, blank], axis=1)
        target_parent = jnp.concatenate([blank, jnp.zeros((1, 2 * rims), i32), own_near], axis=1)
        line = lax.broadcasted_iota(i32, (table_v.shape[0] - features, table_v.shape[1]), 0)
        named = jnp.where(line == 0, source_parent, jnp.where(line == 1, target_parent, 0))
        table_v[features:] = named.astype(f32).astype(bf16)
        lift_v[...] = one_hot(as_columns(own_near, lift_v.shape[1]), 1, lift_v.shape)

    step = next(size for size in (512, 256, 128) if edges % size == 0)

    def known(i):
        span = pl.ds(i * step, step)
        source_pick = one_hot(edge_ids_v[0, :, span], 0, (fines + 2 * rims, step))
        target_pick = one_hot(edge_ids_v[1, :, span], 0, (fines, step))
        target_v[:, span] = target_pick
        found = product(table_v[...], jnp.concatenate([source_pick, target_pick], axis=0))
        known_v[:, span] = found[:features].astype(bf16)
        source_near = found[features : features + 1].astype(i32)
        target_near = found[features + 1 : features + 2].astype(i32) + 5 * mids
        line = lax.broadcasted_iota(i32, (8 * mids, step), 0)
        lookup_v[:, span] = jnp.where((line == source_near) | (line == target_near), 1.0, 0.0).astype(bf16)

    blocks_of_edges = iter(range(edges // step))

    def do_known(n=1):
        await_load("edges")
        for i in [i for _, i in zip(range(n), blocks_of_edges)]:
            known(i)

    def coarse_part(ns, cores):
        places = [(heights[n], c) for c in cores for n in ns]
        blocks = [ups_ref[pl.ds(place_of(h, 0, c), pairs)].reshape(pairs * mids, features) for h, c in places]
        slots = [id_place_of(h, p, c) for h, c in places for p in range(pairs)]
        id_row = jnp.concatenate([ids_ref[slot][:, :mids] for slot in slots], axis=1)
        picker = one_hot(id_row, 0, (coarse_count, len(slots) * mids))
        return product(picker, jnp.concatenate(blocks, axis=0))

    nearby = []
    for d in range(-2, 3):
        other = (me + d + 2 * groups * tiles) % (groups * tiles)
        other_tile = other % tiles
        nearby.append((other // tiles, other_tile // 2, other_tile % 2))

    def find_near():
        window, padded = pick_v.shape
        spare = ceil(window) - window
        near_row = jnp.concatenate([ids_ref[id_place_of(*place)][:, :mids] for place in nearby] + [jnp.zeros((1, spare), i32)], axis=1)
        pick_v[...] = one_hot(as_columns(near_row, padded)[:window], 1, (window, padded))

    def column_rows(place):
        return ups_ref[pl.ds(place, groups)].reshape(groups * mids, features)

    def column_at(n):
        arrive(place_of(heights[n], pair, core), 1, n)
        spread(n)

    def across_at(n):
        arrive(0, len(level), groups + n)
        for other in level:
            send(other, n, [partner], 2 * groups + n)

    def partner_at(n):
        arrive(place_of(heights[n], 0, 1 - core), pairs, 2 * groups + n)

    columns_left = iter(range(1, groups))
    across_left = iter(range(groups))

    def relay(left, step_at, n=1):
        for i in [i for _, i in zip(range(n), left)]:
            step_at(i)

    keep_message()
    ids_across()
    fill_table()
    do_known()
    relay(columns_left, column_at)
    do_known()
    relay(columns_left, column_at)
    keep_coarse()
    relay(columns_left, column_at, groups)
    do_known()
    relay(across_left, across_at)
    ids_partner()
    do_known()
    keep_ending()
    keep_first()
    relay(across_left, across_at)
    do_known()
    relay(across_left, across_at)
    ids_done()
    find_near()
    early = range(groups - 1)
    gained_v[...] = coarse_part(early, [core])
    relay(across_left, across_at, groups)
    do_known(edges)
    for n in early:
        partner_at(n)
    gained_v[...] += coarse_part(early, [1 - core])
    partner_at(groups - 1)
    gained_v[...] += coarse_part([groups - 1], [core, 1 - core])
    near_v[...] = jnp.concatenate([ups_ref[place_of(*place)] for place in nearby], axis=0)

    @pl.when(tile > 0)
    def _():
        for copy in to_before:
            copy.wait_send()

    @pl.when(tile < tiles - 1)
    def _():
        for copy in to_after:
            copy.wait_send()

    total = sum(ids_sent)
    for first in range(0, total, ids_ref.shape[0]):
        sent = ids_ref.at[pl.ds(0, min(total - first, ids_ref.shape[0]))]
        pltpu.make_async_copy(sent, sent, id_send.at[0]).wait()
    for first in range(0, len(started), ups_ref.shape[0]):
        blocks = ups_ref.at[pl.ds(0, min(len(started) - first, ups_ref.shape[0]))]
        pltpu.make_async_copy(blocks, blocks, tree_send.at[0]).wait()
    await_load("handed")


def finish_kernel(*refs):
    pre_v, known_v, lookup_v, target_v, first_v, fine_v, coarse_v = refs[:7]
    near_v, pick_v, lift_v, flip_v, ending_v, handed_v, message_v, gained_v = refs[7:15]
    fine_out_ref, mid_out_ref, coarse_out_ref = refs[15:18]
    fine_out_v, mid_out_v, coarse_out_v, padded_v, sums_v, out_sem = refs[18:]
    window, padded = pick_v.shape
    mids = mid_out_v.shape[0]
    fines, features = fine_v.shape
    coarse_count = coarse_v.shape[0]
    edges = known_v.shape[1]
    weights = {name: handed_v.at[i] for i, name in enumerate(FINISH_WEIGHTS)}
    outs = []

    def put(source, target):
        outs.append(pltpu.make_async_copy(source, target, out_sem.at[len(outs)]))
        outs[-1].start()

    hidden = gate(pre_v[...] + product(gained_v[...].astype(bf16), message_v[...])).astype(bf16)
    updated = (coarse_v[...].astype(f32) + normed(product(hidden, weights["coarse_w3"][...]))).astype(bf16)
    coarse_out_v[...] = updated
    put(coarse_out_v, coarse_out_ref)
    edge = coarse_count // 16 * 16
    padded_v[edge:] = jnp.zeros((padded - edge, features), bf16)
    padded_v[:coarse_count] = updated

    picked = product(pick_v[...], padded_v[...]).astype(bf16)
    down = product(picked, weights["w_descend"][...])
    near_out = (near_v[...].astype(f32) + down).astype(bf16)
    mid_out_v[...] = near_out[2 * mids : 3 * mids]
    put(mid_out_v, mid_out_ref)
    fine_down = product(near_out, weights["w_fine"][...]).astype(bf16)
    beside = fine_down[mids : 4 * mids]

    def blank(rows):
        return jnp.zeros((rows, features), bf16)

    source_rows = jnp.concatenate([fine_down, blank(3 * mids)], axis=0)
    target_rows = jnp.concatenate([blank(5 * mids), beside], axis=0)
    change = (flipped(flip_v[0], source_rows) + flipped(flip_v[1], target_rows)).astype(bf16)

    step = next(size for size in (1024, 512, 256, 128) if edges % size == 0)
    total = None
    for i in range(edges // step):
        span = slice(i * step, (i + 1) * step)
        edge_sum = product(change, lookup_v[:, span]) + known_v[:, span].astype(f32)
        part = flipped(target_v[:, span], gate(edge_sum).astype(bf16))
        if i == 0:
            sums_v[...] = part
        else:
            sums_v[...] += part

    spare = lift_v.shape[1] - 3 * mids
    beside_first = product(beside, weights["node_w1"][...]).astype(bf16)
    lift = lift_v[...]
    if spare:
        beside = jnp.concatenate([beside, blank(spare)], axis=0)
        beside_first = jnp.concatenate([beside_first, blank(spare)], axis=0)
    lifted = (fine_v[...].astype(f32) + product(lift, beside)).astype(bf16)
    incoming = first_v[...] + product(lift, beside_first)
    incoming += product(sums_v[...].astype(bf16), ending_v[...])
    hidden = gate(incoming).astype(bf16)
    rows = fines // 2
    for half in range(2):
        span = slice(half * rows, (half + 1) * rows)
        result = lifted[span].astype(f32) + normed(product(hidden[span], weights["node_w3"][...]))
        fine_out_v[span] = result.astype(bf16)
        put(fine_out_v.at[span], fine_out_ref.at[span])
    for copy in outs:
        copy.wait()


def on_device(
    fine_latent,
    mid_latent,
    coarse_latent,
    fine_parent,
    mid_parent,
    halo_rows,
    edge_source,
    edge_target,
    w_child,
    mid_w1,
    mid_w2,
    mid_w3,
    w_coarse,
    coarse_w1,
    coarse_w2,
    coarse_w3,
    w_descend,
    w_fine,
    edge_w_src,
    edge_w_dst,
    edge_w2,
    node_w1,
    node_w2,
    node_w3,
):
    named = dict(
        w_child=w_child,
        mid_w1=mid_w1,
        mid_w2=mid_w2,
        mid_w3=mid_w3,
        w_coarse=w_coarse,
        coarse_w1=coarse_w1,
        coarse_w2=coarse_w2,
        coarse_w3=coarse_w3,
        w_descend=w_descend,
        w_fine=w_fine,
        edge_w_src=edge_w_src,
        edge_w_dst=edge_w_dst,
        edge_w2=edge_w2,
        node_w1=node_w1,
        node_w2=node_w2,
        node_w3=node_w3,
    )
    groups, tiles = (lax.axis_size("rhombus"), lax.axis_size("tile"))
    devices = groups * tiles
    fines, features = fine_latent.shape
    mids = mid_latent.shape[0]
    halos = halo_rows.shape[0]
    rims = halos // 2
    edges = edge_source.shape[0]
    coarse_count = coarse_latent.shape[0]
    width = ceil(mids)
    pairs = tiles // 2
    vmem = pl.BlockSpec(memory_space=pltpu.VMEM)
    hbm = pl.BlockSpec(memory_space=pl.ANY)
    dma = pltpu.SemaphoreType.DMA
    square = (features, features)
    small = [fine_parent[None, :], halo_rows[None, :], mid_parent[None, :], mid_latent]
    edge_ids = [edge_source[None, :], edge_target[None, :]]
    weights = [named[name] for name in GATHER_WEIGHTS + FINISH_WEIGHTS]
    handed = (
        pltpu.VMEM((coarse_count, features), f32),
        pltpu.VMEM((features, edges), bf16),
        pltpu.VMEM((8 * mids, edges), bf16),
        pltpu.VMEM((fines, edges), bf16),
        pltpu.VMEM((fines, features), f32),
        pltpu.VMEM((fines, features), bf16),
        pltpu.VMEM((coarse_count, features), bf16),
        pltpu.VMEM((5 * mids, features), bf16),
        pltpu.VMEM((5 * mids, ceil(coarse_count)), bf16),
        pltpu.VMEM((fines, ceil(3 * mids)), bf16),
        pltpu.VMEM((2, *square), bf16),
        pltpu.VMEM(square, bf16),
        pltpu.VMEM((len(FINISH_WEIGHTS), *square), bf16),
        pltpu.VMEM(square, bf16),
        pltpu.VMEM((coarse_count, features), f32),
    )
    between = pl.pallas_call(
        lambda *refs: gather_kernel(groups, tiles, *refs),
        out_shape=handed,
        in_specs=[hbm] * (len(small) + 4 + len(weights)),
        out_specs=(vmem,) * len(handed),
        scratch_shapes=[
            pltpu.VMEM((devices, mids, features), bf16),
            pltpu.VMEM((devices, 1, width), i32),
            pltpu.VMEM((halos, features), bf16),
            pltpu.VMEM((2, 1, rims), i32),
            pltpu.VMEM((len(GATHER_WEIGHTS), *square), bf16),
            *[pltpu.VMEM(array.shape, array.dtype) for array in small],
            pltpu.VMEM((2, 1, edges), i32),
            pltpu.VMEM((2, mids, features), bf16),
            pltpu.VMEM((2, mids, features), bf16),
            pltpu.VMEM((halos, features), bf16),
            pltpu.VMEM((2, 1, rims), i32),
            pltpu.VMEM((features + 16, 2 * fines + halos), bf16),
            dma((len(small) + 5 + len(LOADS),)),
            dma((6,)),
            dma((6,)),
            dma((1,)),
            dma((3 * groups,)),
            dma((1,)),
            dma((pairs + 1,)),
        ],
        compiler_params=pltpu.CompilerParams(collective_id=0, has_side_effects=True, vmem_limit_bytes=40 << 20),
        name="sweep_gather",
    )(*small, *edge_ids, fine_latent, coarse_latent, *weights)
    return pl.pallas_call(
        finish_kernel,
        out_shape=(
            jax.ShapeDtypeStruct((fines, features), bf16),
            jax.ShapeDtypeStruct((mids, features), bf16),
            jax.ShapeDtypeStruct((coarse_count, features), bf16),
        ),
        in_specs=[vmem] * len(handed),
        out_specs=(hbm,) * 3,
        scratch_shapes=[
            pltpu.VMEM((fines, features), bf16),
            pltpu.VMEM((mids, features), bf16),
            pltpu.VMEM((coarse_count, features), bf16),
            pltpu.VMEM((ceil(coarse_count), features), bf16),
            pltpu.VMEM((fines, features), f32),
            dma((4,)),
        ],
        compiler_params=pltpu.CompilerParams(vmem_limit_bytes=24 << 20),
        name="sweep_finish",
    )(*between)


def solution(mesh):
    split, rows, whole = (P(("rhombus", "tile")), P(("rhombus", "tile"), None), P())
    placed = (rows, rows, whole) + (split,) * 5 + (whole,) * 16
    return jax.shard_map(
        on_device,
        mesh=mesh,
        in_specs=placed,
        out_specs=(rows, rows, whole),
        check_vma=False,
    )
```

```python
import jax
import jax.numpy as jnp
from jax import lax
from jax.experimental import pallas as pl
from jax.experimental.pallas import tpu as pltpu
from jax.sharding import PartitionSpec as P

MESH = pl.DeviceIdType.MESH

EPSILON = 1e-05

bf16, f32, i32 = (jnp.bfloat16, jnp.float32, jnp.int32)

ACROSS = (((1,), (1,)), ((), ()))


def product(left, right):
    return jnp.dot(left, right, preferred_element_type=f32)


def flipped(left, right):
    return lax.dot_general(left, right, ACROSS, preferred_element_type=f32)


def normed(values):
    return values / jnp.sqrt(jnp.mean(values * values, axis=-1, keepdims=True) + EPSILON)


def gate(values):
    return values * (0.5 + 0.5 * jnp.tanh(0.5 * values))


def one_hot(ids, axis, shape):
    line = lax.broadcasted_iota(jnp.int16, shape, axis)
    return jnp.where(line == ids.astype(jnp.int16), jnp.ones((), bf16), jnp.zeros((), bf16))


def as_columns(row, width):
    count = row.shape[1]
    column = jnp.transpose(jnp.broadcast_to(row, (128, count)))
    return jnp.concatenate([column] * (width // 128), axis=1)


def ceil(n, unit=128):
    return -(-n // unit) * unit


GATHER_WEIGHTS = (
    "w_child",
    "mid_w2",
    "mid_w1",
    "mid_w3",
    "edge_w_dst",
    "edge_w_src",
    "w_coarse",
    "coarse_w2",
    "coarse_w1",
)
FINISH_WEIGHTS = ("coarse_w3", "edge_w2", "node_w2", "w_descend", "w_fine", "node_w1", "node_w3")
EARLY = 0
BY_HEIGHT = (1, 2)
SMALL = ("parent", "halo", "coarse_id", "latent")
LOADS = (2, 2, 1, 1, 2, 1)


def gather_kernel(groups, tiles, *refs):
    refs = iter(refs)

    def take(n):
        return [next(refs) for _ in range(n)]

    small_refs = dict(zip(SMALL + ("source", "target"), take(len(SMALL) + 2)))
    fine_ref, coarse_ref = take(2)
    weight_refs = dict(zip(GATHER_WEIGHTS + FINISH_WEIGHTS, take(len(GATHER_WEIGHTS + FINISH_WEIGHTS))))
    pre_v, known_v, lookup_v, target_v, fine_v, coarse_v = take(6)
    near_v, pick_v, lift_v, flip_v, handed_v, message_v, gained_v = take(7)
    ups_ref, ids_ref, rim_ref, rim_parent_ref, weights_v = take(5)
    small_v = dict(zip(SMALL, take(len(SMALL))))
    (edge_ids_v,) = take(1)
    side_v, beside_v, picked_v, picked_parent_v, table_v, target_near_v = take(6)
    load_sem, near_send, near_recv, tree_send, block_recv, id_send, id_recv = take(7)

    group, tile = (lax.axis_index("rhombus"), lax.axis_index("tile"))
    pairs = tiles // 2
    pair, core = (tile // 2, tile % 2)
    mids = small_v["latent"].shape[0]
    rims = small_v["halo"].shape[1] // 2
    fines, features = fine_v.shape
    coarse_count = coarse_v.shape[0]
    edges = edge_ids_v.shape[2]

    def at(group_id, pair_id, core_id):
        return (group_id, pair_id * 2 + core_id)

    if groups == 4:
        heights = [group, group + 1 - 2 * (group % 2), (group + 2) % 4, 3 - group]
    else:
        order = [0] + sorted(range(1, groups), key=lambda k: min(k, groups - k))
        heights = [(group + k) % groups for k in order]
    columns = [at(height, pair, core) for height in heights[1:]]
    if pairs == 4:
        beside = pair + 1 - 2 * (pair % 2)
        level = [beside, (pair + 2) % 4, (beside + 2) % 4]
        around = BY_HEIGHT if groups == 4 else ()
    else:
        level = [(pair + k) % pairs for k in range(1, pairs)]
        around = ()
    row_peers = [at(group, other, core) for other in level]
    partner = at(group, pair, 1 - core)
    peers = columns + row_peers + [partner]

    barrier = pltpu.get_barrier_semaphore()
    for peer in peers:
        pl.semaphore_signal(barrier, inc=1, device_id=peer, device_id_type=MESH)

    @pl.when(tile > 0)
    def _():
        pl.semaphore_signal(barrier, inc=1, device_id=(group, tile - 1), device_id_type=MESH)

    @pl.when(tile < tiles - 1)
    def _():
        pl.semaphore_signal(barrier, inc=1, device_id=(group, tile + 1), device_id_type=MESH)

    loads = {}

    def load(name, *pairs_of_refs, whole=None):
        sem = load_sem.at[len(loads)]
        for source, held in pairs_of_refs:
            pltpu.make_async_copy(source, held, sem).start()
        held = pairs_of_refs[0][1] if whole is None else whole
        loads[name] = pltpu.make_async_copy(held, held, sem)

    load("parent", (small_refs["parent"], small_v["parent"]))
    load("fine", (fine_ref, fine_v))
    for name in ("halo", "latent", "coarse_id"):
        load(name, (small_refs[name], small_v[name]))
    held = {name: weights_v.at[i] for i, name in enumerate(GATHER_WEIGHTS)}
    held.update({name: handed_v.at[i] for i, name in enumerate(FINISH_WEIGHTS)})
    first = 0
    for n, count in enumerate(LOADS):
        names = GATHER_WEIGHTS[first : first + count]
        load(n, *[(weight_refs[name], held[name]) for name in names], whole=weights_v.at[pl.ds(first, count)])
        first += count
        if n == 1:
            ids = [(small_refs[name], edge_ids_v.at[i]) for i, name in enumerate(("source", "target"))]
            load("edges", *ids, whole=edge_ids_v)
        if n == 4:
            load("coarse", (coarse_ref, coarse_v))
    load("handed", *[(weight_refs[name], held[name]) for name in FINISH_WEIGHTS], whole=handed_v)
    waited = set()

    def await_load(name):
        if name not in waited:
            loads[name].wait()
            waited.add(name)

    def weight(name):
        place = GATHER_WEIGHTS.index(name)
        await_load(next(n for n in range(len(LOADS)) if place < sum(LOADS[: n + 1])))
        return held[name][...]

    me = group * tiles + tile
    halves = groups * pairs

    def place_of(group_id, pair_id, core_id):
        return core_id * halves + group_id * pairs + pair_id

    def id_place_of(group_id, pair_id, core_id):
        return core_id * halves + pair_id * groups + group_id

    mine = place_of(group, pair, core)
    await_load("parent")
    parents = small_v["parent"][...]
    picker = one_hot(parents, 0, (3 * mids, fines))
    await_load("fine")
    sums = product(picker, fine_v[...])
    side_v[0] = sums[mids : 2 * mids].astype(bf16)
    side_v[1] = sums[2 * mids :].astype(bf16)
    pl.semaphore_wait(barrier, len(peers) + 1 + (tile + tiles - 1) // tiles - (tile + 1) // tiles)

    def near(index, source, target, device):
        return pltpu.make_async_remote_copy(
            src_ref=source,
            dst_ref=target,
            send_sem=near_send.at[index],
            recv_sem=near_recv.at[index],
            device_id=device,
            device_id_type=MESH,
        )

    before, after = ((group, tile - 1), (group, tile + 1))
    to_before = [
        near(0, side_v.at[0], beside_v.at[0], before),
        near(1, picked_v.at[pl.ds(0, rims)], rim_ref.at[pl.ds(rims, rims)], before),
        near(2, picked_parent_v.at[0], rim_parent_ref.at[1], before),
    ]
    to_after = [
        near(3, side_v.at[1], beside_v.at[1], after),
        near(4, picked_v.at[pl.ds(rims, rims)], rim_ref.at[pl.ds(0, rims)], after),
        near(5, picked_parent_v.at[1], rim_parent_ref.at[0], after),
    ]

    @pl.when(tile > 0)
    def _():
        to_before[0].start()

    @pl.when(tile < tiles - 1)
    def _():
        to_after[0].start()

    ids_sent = []

    def pass_ids(first_slot, count, device, kind):
        copy = pltpu.make_async_remote_copy(
            src_ref=ids_ref.at[pl.ds(first_slot, count)],
            dst_ref=ids_ref.at[pl.ds(first_slot, count)],
            send_sem=id_send.at[0],
            recv_sem=id_recv.at[kind],
            device_id=device,
            device_id_type=MESH,
        )
        copy.start()
        ids_sent.append(count)

    def await_ids(first_slot, count, kind):
        held_ids = ids_ref.at[pl.ds(first_slot, count)]
        pltpu.make_async_copy(held_ids, held_ids, id_recv.at[kind]).wait()

    def column_of(pair_id, core_id):
        return id_place_of(0, pair_id, core_id)

    await_load("coarse_id")
    spare_ids = jnp.zeros((1, ids_ref.shape[2] - mids), i32)
    my_id = id_place_of(group, pair, core)
    ids_ref[my_id] = jnp.concatenate([small_v["coarse_id"][...], spare_ids], axis=1)
    for device in columns:
        pass_ids(my_id, 1, device, 0)

    def ids_across():
        await_ids(0, groups - 1, 0)
        for n, device in enumerate(row_peers):
            pass_ids(column_of(pair, core), groups, device, 1 + n)

    def ids_partner():
        for n, other in enumerate(level):
            await_ids(column_of(other, core), groups, 1 + n if pairs == 4 else len(level) - n)
        pass_ids(core * halves, halves, partner, len(level) + 1)

    def ids_done():
        await_ids((1 - core) * halves, halves, len(level) + 1)

    await_load("halo")
    halo = small_v["halo"][...]
    picked_v[...] = product(one_hot(as_columns(halo, fines), 1, (2 * rims, fines)), fine_v[...]).astype(bf16)
    side = parents // mids
    shift = jnp.where(side == 1, -1, jnp.where(side == 2, 1, 0))
    within = parents % mids
    parent_column = jnp.transpose(jnp.broadcast_to((me + shift) * mids + within, (128, fines)))
    for half in range(2):
        hit = lax.broadcasted_iota(i32, (fines, rims), 0) == halo[:, half * rims : (half + 1) * rims]
        spread = jnp.concatenate([parent_column] * (rims // 128), axis=1)
        picked_parent_v[half] = jnp.sum(jnp.where(hit, spread, 0), axis=0, keepdims=True)

    @pl.when(tile > 0)
    def _():
        to_before[1].start()
        to_before[2].start()

    @pl.when(tile < tiles - 1)
    def _():
        to_after[1].start()
        to_after[2].start()

    child_mid = product(weight("w_child"), weight("mid_w2")).astype(bf16)
    await_load("latent")
    kept_mid = product(small_v["latent"][...], weight("mid_w1"))
    flip_v[1] = jnp.transpose(weight("edge_w_dst"))
    table_v[:features, fines + 2 * rims :] = flipped(flip_v[1], fine_v[...]).astype(bf16)
    flip_v[0] = jnp.transpose(weight("edge_w_src"))
    table_v[:features, :fines] = flipped(flip_v[0], fine_v[...]).astype(bf16)
    own_near = (1 + shift) * mids + within
    step = next(size for size in (512, 256, 128) if edges % size == 0)
    sources = fines + 2 * rims
    line = lax.broadcasted_iota(i32, (table_v.shape[0] - features, fines), 0)
    table_v[features:, sources:] = jnp.where(line == 1, own_near, 0).astype(f32).astype(bf16)

    def known_target(i):
        span = pl.ds(i * step, step)
        target_pick = one_hot(edge_ids_v[1, :, span], 0, (fines, step))
        target_v[:, span] = target_pick
        found = product(table_v[:, sources:], target_pick)
        known_v[:, span] = found[:features].astype(bf16)
        target_near_v[:, span] = found[features + 1 : features + 2].astype(i32)

    def known(i):
        span = pl.ds(i * step, step)
        source_pick = one_hot(edge_ids_v[0, :, span], 0, (sources, step))
        if i < EARLY:
            found = product(table_v[:, :sources], source_pick)
            known_v[:, span] = (found[:features] + known_v[:, span].astype(f32)).astype(bf16)
            target_near = target_near_v[:, span]
        else:
            target_pick = one_hot(edge_ids_v[1, :, span], 0, (fines, step))
            target_v[:, span] = target_pick
            found = product(table_v[...], jnp.concatenate([source_pick, target_pick], axis=0))
            known_v[:, span] = found[:features].astype(bf16)
            target_near = found[features + 1 : features + 2].astype(i32)
        source_near = found[features : features + 1].astype(i32)
        line = lax.broadcasted_iota(i32, (8 * mids, step), 0)
        hit = (line == source_near) | (line == target_near + 5 * mids)
        lookup_v[:, span] = jnp.where(hit, 1.0, 0.0).astype(bf16)

    await_load("edges")
    for i in range(EARLY):
        known_target(i)
    mid_w3 = weight("mid_w3")

    @pl.when(tile > 0)
    def _():
        to_after[0].wait_recv()

    @pl.when(tile == 0)
    def _():
        beside_v[1] = jnp.zeros_like(beside_v[1])
        rim_ref[pl.ds(0, rims)] = jnp.zeros((rims, features), bf16)
        rim_parent_ref[0] = jnp.full(rim_parent_ref.shape[1:], -1, i32)

    @pl.when(tile < tiles - 1)
    def _():
        to_before[0].wait_recv()

    @pl.when(tile == tiles - 1)
    def _():
        beside_v[0] = jnp.zeros_like(beside_v[0])
        rim_ref[pl.ds(rims, rims)] = jnp.zeros((rims, features), bf16)
        rim_parent_ref[1] = jnp.full(rim_parent_ref.shape[1:], -1, i32)

    total = (sums[:mids] + beside_v[0].astype(f32) + beside_v[1].astype(f32)).astype(bf16)
    hidden = gate(kept_mid + product(total, child_mid)).astype(bf16)
    mid_up = small_v["latent"][...].astype(f32) + normed(product(hidden, mid_w3))
    ups_ref[mine] = mid_up.astype(bf16)

    started = []

    def send(pair_id, n, devices, recv):
        slot = place_of(heights[n], pair_id, core)
        for device in devices:
            copy = pltpu.make_async_remote_copy(
                src_ref=ups_ref.at[slot],
                dst_ref=ups_ref.at[slot],
                send_sem=tree_send.at[0],
                recv_sem=block_recv.at[recv],
                device_id=device,
                device_id_type=MESH,
            )
            copy.start()
            started.append(copy)

    def arrive(first_slot, count, recv):
        blocks = ups_ref.at[pl.ds(first_slot, count)]
        pltpu.make_async_copy(blocks, blocks, block_recv.at[recv]).wait()

    def place_in(n):
        return n if groups == 4 else order.index((groups - order[n]) % groups)

    def spread(n):
        send(pair, n, row_peers[:-1] if n in around else row_peers, groups + n)
        send(pair, n, [partner], 2 * groups + n)

    for n in range(1, groups):
        send(pair, 0, [columns[n - 1]], place_in(n))
        if n == 1:
            spread(0)


    def keep_coarse():
        await_load("coarse")
        pre_v[...] = product(coarse_v[...], weight("coarse_w1"))

    def keep_message():
        message_v[...] = product(weight("w_coarse"), weight("coarse_w2")).astype(bf16)

    def fill_table():
        @pl.when(tile > 0)
        def _():
            for copy in to_after[1:]:
                copy.wait_recv()

        @pl.when(tile < tiles - 1)
        def _():
            for copy in to_before[1:]:
                copy.wait_recv()

        table_v[:features, fines : fines + 2 * rims] = flipped(flip_v[0], rim_ref[...]).astype(bf16)
        far = jnp.concatenate([rim_parent_ref[0], rim_parent_ref[1]], axis=1)
        far = jnp.where(far < 0, -1, far - (me - 2) * mids)
        source_parent = jnp.concatenate([own_near + mids, far], axis=1)
        line = lax.broadcasted_iota(i32, (table_v.shape[0] - features, sources), 0)
        table_v[features:, :sources] = jnp.where(line == 0, source_parent, 0).astype(f32).astype(bf16)
        lift_v[...] = one_hot(as_columns(own_near, lift_v.shape[1]), 1, lift_v.shape)

    blocks_of_edges = iter(range(edges // step))

    def do_known(n=1):
        for i in [i for _, i in zip(range(n), blocks_of_edges)]:
            known(i)

    def coarse_part(pieces):
        places = [(heights[n], c) for n, c in pieces]
        blocks = [ups_ref[pl.ds(place_of(h, 0, c), pairs)].reshape(pairs * mids, features) for h, c in places]
        slots = [id_place_of(h, p, c) for h, c in places for p in range(pairs)]
        id_row = jnp.concatenate([ids_ref[slot][:, :mids] for slot in slots], axis=1)
        picker = one_hot(id_row, 0, (coarse_count, len(slots) * mids))
        return product(picker, jnp.concatenate(blocks, axis=0))

    nearby = []
    for d in range(-2, 3):
        other = (me + d + 2 * groups * tiles) % (groups * tiles)
        other_tile = other % tiles
        nearby.append((other // tiles, other_tile // 2, other_tile % 2))

    def find_near():
        window, padded = pick_v.shape
        spare = ceil(window) - window
        near_row = jnp.concatenate([ids_ref[id_place_of(*place)][:, :mids] for place in nearby] + [jnp.zeros((1, spare), i32)], axis=1)
        pick_v[...] = one_hot(as_columns(near_row, padded)[:window], 1, (window, padded))

    def column_rows(place):
        return ups_ref[pl.ds(place, groups)].reshape(groups * mids, features)

    def column_at(n):
        arrive(place_of(heights[n], pair, core), 1, n)
        spread(n)

    def across_at(n):
        if n in around:
            arrive(0, len(level) - 1, groups + n)
            arrive(0, 1, 3 * groups + n)
        else:
            arrive(0, len(level), groups + n)
        if n == 0:
            for m in around:
                send(level[-1], 0, [columns[m - 1]], 3 * groups + m)
        for other in level:
            send(other, n, [partner], 2 * groups + n)

    def partner_at(n):
        arrive(place_of(heights[n], 0, 1 - core), pairs, 2 * groups + n)

    columns_left = iter(range(1, groups))
    across_left = iter(range(groups))

    def relay(left, step_at, n=1):
        for i in [i for _, i in zip(range(n), left)]:
            step_at(i)

    keep_message()
    ids_across()
    fill_table()
    do_known(1)
    keep_coarse()
    relay(columns_left, column_at)
    do_known(1)
    relay(columns_left, column_at)
    relay(across_left, across_at)
    relay(columns_left, column_at, groups)
    ids_partner()
    do_known(3)
    relay(across_left, across_at)
    relay(across_left, across_at)
    ids_done()
    find_near()
    gained_v[...] = coarse_part([(n, core) for n in range(groups - 1)])
    relay(across_left, across_at, groups)
    do_known(edges)
    for n in range(groups):
        partner_at(n)
    gained_v[...] += coarse_part([(groups - 1, core)] + [(n, 1 - core) for n in range(groups)])
    near_v[...] = jnp.concatenate([ups_ref[place_of(*place)] for place in nearby], axis=0)

    @pl.when(tile > 0)
    def _():
        for copy in to_before:
            copy.wait_send()

    @pl.when(tile < tiles - 1)
    def _():
        for copy in to_after:
            copy.wait_send()

    total = sum(ids_sent)
    for first in range(0, total, ids_ref.shape[0]):
        sent = ids_ref.at[pl.ds(0, min(total - first, ids_ref.shape[0]))]
        pltpu.make_async_copy(sent, sent, id_send.at[0]).wait()
    for first in range(0, len(started), ups_ref.shape[0]):
        blocks = ups_ref.at[pl.ds(0, min(len(started) - first, ups_ref.shape[0]))]
        pltpu.make_async_copy(blocks, blocks, tree_send.at[0]).wait()
    await_load("handed")


def finish_kernel(*refs):
    pre_v, known_v, lookup_v, target_v, fine_v, coarse_v = refs[:6]
    near_v, pick_v, lift_v, flip_v, handed_v, message_v, gained_v = refs[6:13]
    fine_out_ref, mid_out_ref, coarse_out_ref = refs[13:16]
    fine_out_v, mid_out_v, coarse_out_v, padded_v, sums_v, first_v, ending_v, out_sem = refs[16:]
    window, padded = pick_v.shape
    mids = mid_out_v.shape[0]
    fines, features = fine_v.shape
    coarse_count = coarse_v.shape[0]
    edges = known_v.shape[1]
    weights = {name: handed_v.at[i] for i, name in enumerate(FINISH_WEIGHTS)}
    outs = []

    def put(source, target):
        outs.append(pltpu.make_async_copy(source, target, out_sem.at[len(outs)]))
        outs[-1].start()

    quarter = features // 4
    fills = iter(range(8))

    def fill(n=1):
        for i in [i for _, i in zip(range(n), fills)]:
            part = slice(i % 4 * quarter, (i % 4 + 1) * quarter)
            if i < 4:
                ending_v[part] = product(weights["edge_w2"][part], weights["node_w2"][...]).astype(bf16)
            else:
                rows = slice(i % 4 * fines // 4, (i % 4 + 1) * fines // 4)
                first_v[rows] = product(fine_v[rows], weights["node_w1"][...])

    message = product(gained_v[...].astype(bf16), message_v[...])
    fill(2)
    hidden = gate(pre_v[...] + message).astype(bf16)
    change_out = product(hidden, weights["coarse_w3"][...])
    fill(2)
    updated = (coarse_v[...].astype(f32) + normed(change_out)).astype(bf16)
    coarse_out_v[...] = updated
    put(coarse_out_v, coarse_out_ref)
    edge = coarse_count // 16 * 16
    padded_v[edge:] = jnp.zeros((padded - edge, features), bf16)
    padded_v[:coarse_count] = updated

    picked = product(pick_v[...], padded_v[...]).astype(bf16)
    fill()
    down = product(picked, weights["w_descend"][...])
    fill()
    near_out = (near_v[...].astype(f32) + down).astype(bf16)
    mid_out_v[...] = near_out[2 * mids : 3 * mids]
    put(mid_out_v, mid_out_ref)
    fine_down = product(near_out, weights["w_fine"][...]).astype(bf16)
    fill(8)
    beside = fine_down[mids : 4 * mids]

    def blank(rows):
        return jnp.zeros((rows, features), bf16)

    source_rows = jnp.concatenate([fine_down, blank(3 * mids)], axis=0)
    target_rows = jnp.concatenate([blank(5 * mids), beside], axis=0)
    change = (flipped(flip_v[0], source_rows) + flipped(flip_v[1], target_rows)).astype(bf16)

    step = next(size for size in (1024, 512, 256, 128) if edges % size == 0)
    spare = lift_v.shape[1] - 3 * mids
    beside_first = product(beside, weights["node_w1"][...]).astype(bf16)
    lift = lift_v[...]
    if spare:
        beside = jnp.concatenate([beside, blank(spare)], axis=0)
        beside_first = jnp.concatenate([beside_first, blank(spare)], axis=0)
    lifted = (fine_v[...].astype(f32) + product(lift, beside)).astype(bf16)
    incoming = first_v[...] + product(lift, beside_first)
    total = None
    for i in range(edges // step):
        span = slice(i * step, (i + 1) * step)
        edge_sum = product(change, lookup_v[:, span]) + known_v[:, span].astype(f32)
        part = flipped(target_v[:, span], gate(edge_sum).astype(bf16))
        if i == 0:
            sums_v[...] = part
        else:
            sums_v[...] += part

    incoming += product(sums_v[...].astype(bf16), ending_v[...])
    hidden = gate(incoming).astype(bf16)
    rows = fines // 2
    for part in range(2):
        span = slice(part * rows, (part + 1) * rows)
        result = lifted[span].astype(f32) + normed(product(hidden[span], weights["node_w3"][...]))
        fine_out_v[span] = result.astype(bf16)
        put(fine_out_v.at[span], fine_out_ref.at[span])
    for copy in outs:
        copy.wait()


def on_device(
    fine_latent,
    mid_latent,
    coarse_latent,
    fine_parent,
    mid_parent,
    halo_rows,
    edge_source,
    edge_target,
    w_child,
    mid_w1,
    mid_w2,
    mid_w3,
    w_coarse,
    coarse_w1,
    coarse_w2,
    coarse_w3,
    w_descend,
    w_fine,
    edge_w_src,
    edge_w_dst,
    edge_w2,
    node_w1,
    node_w2,
    node_w3,
):
    named = dict(
        w_child=w_child,
        mid_w1=mid_w1,
        mid_w2=mid_w2,
        mid_w3=mid_w3,
        w_coarse=w_coarse,
        coarse_w1=coarse_w1,
        coarse_w2=coarse_w2,
        coarse_w3=coarse_w3,
        w_descend=w_descend,
        w_fine=w_fine,
        edge_w_src=edge_w_src,
        edge_w_dst=edge_w_dst,
        edge_w2=edge_w2,
        node_w1=node_w1,
        node_w2=node_w2,
        node_w3=node_w3,
    )
    groups, tiles = (lax.axis_size("rhombus"), lax.axis_size("tile"))
    devices = groups * tiles
    fines, features = fine_latent.shape
    mids = mid_latent.shape[0]
    halos = halo_rows.shape[0]
    rims = halos // 2
    edges = edge_source.shape[0]
    coarse_count = coarse_latent.shape[0]
    width = ceil(mids)
    pairs = tiles // 2
    vmem = pl.BlockSpec(memory_space=pltpu.VMEM)
    hbm = pl.BlockSpec(memory_space=pl.ANY)
    dma = pltpu.SemaphoreType.DMA
    square = (features, features)
    small = [fine_parent[None, :], halo_rows[None, :], mid_parent[None, :], mid_latent]
    edge_ids = [edge_source[None, :], edge_target[None, :]]
    weights = [named[name] for name in GATHER_WEIGHTS + FINISH_WEIGHTS]
    handed = (
        pltpu.VMEM((coarse_count, features), f32),
        pltpu.VMEM((features, edges), bf16),
        pltpu.VMEM((8 * mids, edges), bf16),
        pltpu.VMEM((fines, edges), bf16),
        pltpu.VMEM((fines, features), bf16),
        pltpu.VMEM((coarse_count, features), bf16),
        pltpu.VMEM((5 * mids, features), bf16),
        pltpu.VMEM((5 * mids, ceil(coarse_count)), bf16),
        pltpu.VMEM((fines, ceil(3 * mids)), bf16),
        pltpu.VMEM((2, *square), bf16),
        pltpu.VMEM((len(FINISH_WEIGHTS), *square), bf16),
        pltpu.VMEM(square, bf16),
        pltpu.VMEM((coarse_count, features), f32),
    )
    between = pl.pallas_call(
        lambda *refs: gather_kernel(groups, tiles, *refs),
        out_shape=handed,
        in_specs=[hbm] * (len(small) + 4 + len(weights)),
        out_specs=(vmem,) * len(handed),
        scratch_shapes=[
            pltpu.VMEM((devices, mids, features), bf16),
            pltpu.VMEM((devices, 1, width), i32),
            pltpu.VMEM((halos, features), bf16),
            pltpu.VMEM((2, 1, rims), i32),
            pltpu.VMEM((len(GATHER_WEIGHTS), *square), bf16),
            *[pltpu.VMEM(array.shape, array.dtype) for array in small],
            pltpu.VMEM((2, 1, edges), i32),
            pltpu.VMEM((2, mids, features), bf16),
            pltpu.VMEM((2, mids, features), bf16),
            pltpu.VMEM((halos, features), bf16),
            pltpu.VMEM((2, 1, rims), i32),
            pltpu.VMEM((features + 16, 2 * fines + halos), bf16),
            pltpu.VMEM((1, edges), i32),
            dma((len(small) + 4 + len(LOADS),)),
            dma((6,)),
            dma((6,)),
            dma((1,)),
            dma((4 * groups,)),
            dma((1,)),
            dma((pairs + 1,)),
        ],
        compiler_params=pltpu.CompilerParams(collective_id=0, has_side_effects=True, vmem_limit_bytes=40 << 20),
        name="sweep_gather",
    )(*small, *edge_ids, fine_latent, coarse_latent, *weights)
    return pl.pallas_call(
        finish_kernel,
        out_shape=(
            jax.ShapeDtypeStruct((fines, features), bf16),
            jax.ShapeDtypeStruct((mids, features), bf16),
            jax.ShapeDtypeStruct((coarse_count, features), bf16),
        ),
        in_specs=[vmem] * len(handed),
        out_specs=(hbm,) * 3,
        scratch_shapes=[
            pltpu.VMEM((fines, features), bf16),
            pltpu.VMEM((mids, features), bf16),
            pltpu.VMEM((coarse_count, features), bf16),
            pltpu.VMEM((ceil(coarse_count), features), bf16),
            pltpu.VMEM((fines, features), f32),
            pltpu.VMEM((fines, features), f32),
            pltpu.VMEM(square, bf16),
            dma((6,)),
        ],
        compiler_params=pltpu.CompilerParams(vmem_limit_bytes=24 << 20),
        name="sweep_finish",
    )(*between)


def solution(mesh):
    split, rows, whole = (P(("rhombus", "tile")), P(("rhombus", "tile"), None), P())
    placed = (rows, rows, whole) + (split,) * 5 + (whole,) * 16
    return jax.shard_map(
        on_device,
        mesh=mesh,
        in_specs=placed,
        out_specs=(rows, rows, whole),
        check_vma=False,
    )
```

```python
import jax
import jax.numpy as jnp
from jax import lax
from jax.experimental import pallas as pl
from jax.experimental.pallas import tpu as pltpu
from jax.sharding import PartitionSpec as P

MESH = pl.DeviceIdType.MESH

EPSILON = 1e-05

bf16, f32, i32 = (jnp.bfloat16, jnp.float32, jnp.int32)

ACROSS = (((1,), (1,)), ((), ()))


def product(left, right):
    return jnp.dot(left, right, preferred_element_type=f32)


def flipped(left, right):
    return lax.dot_general(left, right, ACROSS, preferred_element_type=f32)


def normed(values):
    return values / jnp.sqrt(jnp.mean(values * values, axis=-1, keepdims=True) + EPSILON)


def gate(values):
    return values * (0.5 + 0.5 * jnp.tanh(0.5 * values))


def one_hot(ids, axis, shape):
    line = lax.broadcasted_iota(jnp.int16, shape, axis)
    return jnp.where(line == ids.astype(jnp.int16), jnp.ones((), bf16), jnp.zeros((), bf16))


def as_columns(row, width):
    count = row.shape[1]
    column = jnp.transpose(jnp.broadcast_to(row, (128, count)))
    return jnp.concatenate([column] * (width // 128), axis=1)


def ceil(n, unit=128):
    return -(-n // unit) * unit


GATHER_WEIGHTS = (
    "w_child",
    "mid_w2",
    "mid_w1",
    "mid_w3",
    "edge_w_dst",
    "edge_w_src",
    "w_coarse",
    "coarse_w2",
    "coarse_w1",
)
FINISH_WEIGHTS = ("coarse_w3", "edge_w2", "node_w2", "w_descend", "w_fine", "node_w1", "node_w3")
EARLY = 0
BY_HEIGHT = (1, 2, 3)
SMALL = ("parent", "halo", "coarse_id", "latent")
LOADS = (2, 2, 1, 1, 2, 1)


def gather_kernel(groups, tiles, *refs):
    refs = iter(refs)

    def take(n):
        return [next(refs) for _ in range(n)]

    small_refs = dict(zip(SMALL + ("source", "target"), take(len(SMALL) + 2)))
    fine_ref, coarse_ref = take(2)
    weight_refs = dict(zip(GATHER_WEIGHTS + FINISH_WEIGHTS, take(len(GATHER_WEIGHTS + FINISH_WEIGHTS))))
    pre_v, known_v, lookup_v, target_v, fine_v, coarse_v = take(6)
    near_v, pick_v, lift_v, flip_v, handed_v, message_v, gained_v = take(7)
    ups_ref, ids_ref, rim_ref, rim_parent_ref, weights_v = take(5)
    small_v = dict(zip(SMALL, take(len(SMALL))))
    (edge_ids_v,) = take(1)
    side_v, beside_v, picked_v, picked_parent_v, table_v, target_near_v = take(6)
    load_sem, near_send, near_recv, tree_send, block_recv, id_send, id_recv = take(7)

    group, tile = (lax.axis_index("rhombus"), lax.axis_index("tile"))
    pairs = tiles // 2
    pair, core = (tile // 2, tile % 2)
    mids = small_v["latent"].shape[0]
    rims = small_v["halo"].shape[1] // 2
    fines, features = fine_v.shape
    coarse_count = coarse_v.shape[0]
    edges = edge_ids_v.shape[2]

    def at(group_id, pair_id, core_id):
        return (group_id, pair_id * 2 + core_id)

    if groups == 4:
        heights = [group, group + 1 - 2 * (group % 2), (group + 2) % 4, 3 - group]
    else:
        order = [0] + sorted(range(1, groups), key=lambda k: min(k, groups - k))
        heights = [(group + k) % groups for k in order]
    columns = [at(height, pair, core) for height in heights[1:]]
    if pairs == 4:
        beside = pair + 1 - 2 * (pair % 2)
        level = [beside, (pair + 2) % 4, (beside + 2) % 4]
        around = BY_HEIGHT if groups == 4 else ()
    else:
        level = [(pair + k) % pairs for k in range(1, pairs)]
        around = ()
    row_peers = [at(group, other, core) for other in level]
    partner = at(group, pair, 1 - core)
    peers = columns + row_peers + [partner]

    barrier = pltpu.get_barrier_semaphore()
    for peer in peers:
        pl.semaphore_signal(barrier, inc=1, device_id=peer, device_id_type=MESH)

    @pl.when(tile > 0)
    def _():
        pl.semaphore_signal(barrier, inc=1, device_id=(group, tile - 1), device_id_type=MESH)

    @pl.when(tile < tiles - 1)
    def _():
        pl.semaphore_signal(barrier, inc=1, device_id=(group, tile + 1), device_id_type=MESH)

    loads = {}

    def load(name, *pairs_of_refs, whole=None):
        sem = load_sem.at[len(loads)]
        for source, held in pairs_of_refs:
            pltpu.make_async_copy(source, held, sem).start()
        held = pairs_of_refs[0][1] if whole is None else whole
        loads[name] = pltpu.make_async_copy(held, held, sem)

    load("parent", (small_refs["parent"], small_v["parent"]))
    load("fine", (fine_ref, fine_v))
    for name in ("halo", "latent", "coarse_id"):
        load(name, (small_refs[name], small_v[name]))
    held = {name: weights_v.at[i] for i, name in enumerate(GATHER_WEIGHTS)}
    held.update({name: handed_v.at[i] for i, name in enumerate(FINISH_WEIGHTS)})
    first = 0
    for n, count in enumerate(LOADS):
        names = GATHER_WEIGHTS[first : first + count]
        load(n, *[(weight_refs[name], held[name]) for name in names], whole=weights_v.at[pl.ds(first, count)])
        first += count
        if n == 1:
            ids = [(small_refs[name], edge_ids_v.at[i]) for i, name in enumerate(("source", "target"))]
            load("edges", *ids, whole=edge_ids_v)
        if n == 4:
            load("coarse", (coarse_ref, coarse_v))
    load("handed", *[(weight_refs[name], held[name]) for name in FINISH_WEIGHTS], whole=handed_v)
    waited = set()

    def await_load(name):
        if name not in waited:
            loads[name].wait()
            waited.add(name)

    def weight(name):
        place = GATHER_WEIGHTS.index(name)
        await_load(next(n for n in range(len(LOADS)) if place < sum(LOADS[: n + 1])))
        return held[name][...]

    me = group * tiles + tile
    halves = groups * pairs

    def place_of(group_id, pair_id, core_id):
        return core_id * halves + group_id * pairs + pair_id

    def id_place_of(group_id, pair_id, core_id):
        return core_id * halves + pair_id * groups + group_id

    mine = place_of(group, pair, core)
    await_load("parent")
    parents = small_v["parent"][...]
    picker = one_hot(parents, 0, (3 * mids, fines))
    await_load("fine")
    sums = product(picker, fine_v[...])
    side_v[0] = sums[mids : 2 * mids].astype(bf16)
    side_v[1] = sums[2 * mids :].astype(bf16)
    pl.semaphore_wait(barrier, len(peers) + 1 + (tile + tiles - 1) // tiles - (tile + 1) // tiles)

    def near(index, source, target, device):
        return pltpu.make_async_remote_copy(
            src_ref=source,
            dst_ref=target,
            send_sem=near_send.at[index],
            recv_sem=near_recv.at[index],
            device_id=device,
            device_id_type=MESH,
        )

    before, after = ((group, tile - 1), (group, tile + 1))
    to_before = [
        near(0, side_v.at[0], beside_v.at[0], before),
        near(1, picked_v.at[pl.ds(0, rims)], rim_ref.at[pl.ds(rims, rims)], before),
        near(2, picked_parent_v.at[0], rim_parent_ref.at[1], before),
    ]
    to_after = [
        near(3, side_v.at[1], beside_v.at[1], after),
        near(4, picked_v.at[pl.ds(rims, rims)], rim_ref.at[pl.ds(0, rims)], after),
        near(5, picked_parent_v.at[1], rim_parent_ref.at[0], after),
    ]

    @pl.when(tile > 0)
    def _():
        to_before[0].start()

    @pl.when(tile < tiles - 1)
    def _():
        to_after[0].start()

    ids_sent = []

    def pass_ids(first_slot, count, device, kind):
        copy = pltpu.make_async_remote_copy(
            src_ref=ids_ref.at[pl.ds(first_slot, count)],
            dst_ref=ids_ref.at[pl.ds(first_slot, count)],
            send_sem=id_send.at[0],
            recv_sem=id_recv.at[kind],
            device_id=device,
            device_id_type=MESH,
        )
        copy.start()
        ids_sent.append(count)

    def await_ids(first_slot, count, kind):
        held_ids = ids_ref.at[pl.ds(first_slot, count)]
        pltpu.make_async_copy(held_ids, held_ids, id_recv.at[kind]).wait()

    def column_of(pair_id, core_id):
        return id_place_of(0, pair_id, core_id)

    await_load("coarse_id")
    spare_ids = jnp.zeros((1, ids_ref.shape[2] - mids), i32)
    my_id = id_place_of(group, pair, core)
    ids_ref[my_id] = jnp.concatenate([small_v["coarse_id"][...], spare_ids], axis=1)
    for device in columns:
        pass_ids(my_id, 1, device, 0)

    def ids_across():
        await_ids(0, groups - 1, 0)
        for n, device in enumerate(row_peers):
            pass_ids(column_of(pair, core), groups, device, 1 + n)

    def ids_partner():
        for n, other in enumerate(level):
            await_ids(column_of(other, core), groups, 1 + n if pairs == 4 else len(level) - n)
        pass_ids(core * halves, halves, partner, len(level) + 1)

    def ids_done():
        await_ids((1 - core) * halves, halves, len(level) + 1)

    await_load("halo")
    halo = small_v["halo"][...]
    picked_v[...] = product(one_hot(as_columns(halo, fines), 1, (2 * rims, fines)), fine_v[...]).astype(bf16)
    side = parents // mids
    shift = jnp.where(side == 1, -1, jnp.where(side == 2, 1, 0))
    within = parents % mids
    parent_column = jnp.transpose(jnp.broadcast_to((me + shift) * mids + within, (128, fines)))
    for half in range(2):
        hit = lax.broadcasted_iota(i32, (fines, rims), 0) == halo[:, half * rims : (half + 1) * rims]
        spread = jnp.concatenate([parent_column] * (rims // 128), axis=1)
        picked_parent_v[half] = jnp.sum(jnp.where(hit, spread, 0), axis=0, keepdims=True)

    @pl.when(tile > 0)
    def _():
        to_before[1].start()
        to_before[2].start()

    @pl.when(tile < tiles - 1)
    def _():
        to_after[1].start()
        to_after[2].start()

    child_mid = product(weight("w_child"), weight("mid_w2")).astype(bf16)
    await_load("latent")
    kept_mid = product(small_v["latent"][...], weight("mid_w1"))
    flip_v[1] = jnp.transpose(weight("edge_w_dst"))
    table_v[:features, fines + 2 * rims :] = flipped(flip_v[1], fine_v[...]).astype(bf16)
    flip_v[0] = jnp.transpose(weight("edge_w_src"))
    table_v[:features, :fines] = flipped(flip_v[0], fine_v[...]).astype(bf16)
    own_near = (1 + shift) * mids + within
    step = next(size for size in (512, 256, 128) if edges % size == 0)
    sources = fines + 2 * rims
    line = lax.broadcasted_iota(i32, (table_v.shape[0] - features, fines), 0)
    table_v[features:, sources:] = jnp.where(line == 1, own_near, 0).astype(f32).astype(bf16)

    def known_target(i):
        span = pl.ds(i * step, step)
        target_pick = one_hot(edge_ids_v[1, :, span], 0, (fines, step))
        target_v[:, span] = target_pick
        found = product(table_v[:, sources:], target_pick)
        known_v[:, span] = found[:features].astype(bf16)
        target_near_v[:, span] = found[features + 1 : features + 2].astype(i32)

    def known(i):
        span = pl.ds(i * step, step)
        source_pick = one_hot(edge_ids_v[0, :, span], 0, (sources, step))
        if i < EARLY:
            found = product(table_v[:, :sources], source_pick)
            known_v[:, span] = (found[:features] + known_v[:, span].astype(f32)).astype(bf16)
            target_near = target_near_v[:, span]
        else:
            target_pick = one_hot(edge_ids_v[1, :, span], 0, (fines, step))
            target_v[:, span] = target_pick
            found = product(table_v[...], jnp.concatenate([source_pick, target_pick], axis=0))
            known_v[:, span] = found[:features].astype(bf16)
            target_near = found[features + 1 : features + 2].astype(i32)
        source_near = found[features : features + 1].astype(i32)
        line = lax.broadcasted_iota(i32, (8 * mids, step), 0)
        hit = (line == source_near) | (line == target_near + 5 * mids)
        lookup_v[:, span] = jnp.where(hit, 1.0, 0.0).astype(bf16)

    await_load("edges")
    for i in range(EARLY):
        known_target(i)
    mid_w3 = weight("mid_w3")

    @pl.when(tile > 0)
    def _():
        to_after[0].wait_recv()

    @pl.when(tile == 0)
    def _():
        beside_v[1] = jnp.zeros_like(beside_v[1])
        rim_ref[pl.ds(0, rims)] = jnp.zeros((rims, features), bf16)
        rim_parent_ref[0] = jnp.full(rim_parent_ref.shape[1:], -1, i32)

    @pl.when(tile < tiles - 1)
    def _():
        to_before[0].wait_recv()

    @pl.when(tile == tiles - 1)
    def _():
        beside_v[0] = jnp.zeros_like(beside_v[0])
        rim_ref[pl.ds(rims, rims)] = jnp.zeros((rims, features), bf16)
        rim_parent_ref[1] = jnp.full(rim_parent_ref.shape[1:], -1, i32)

    total = (sums[:mids] + beside_v[0].astype(f32) + beside_v[1].astype(f32)).astype(bf16)
    hidden = gate(kept_mid + product(total, child_mid)).astype(bf16)
    mid_up = small_v["latent"][...].astype(f32) + normed(product(hidden, mid_w3))
    ups_ref[mine] = mid_up.astype(bf16)

    started = []

    def send(pair_id, n, devices, recv):
        slot = place_of(heights[n], pair_id, core)
        for device in devices:
            copy = pltpu.make_async_remote_copy(
                src_ref=ups_ref.at[slot],
                dst_ref=ups_ref.at[slot],
                send_sem=tree_send.at[0],
                recv_sem=block_recv.at[recv],
                device_id=device,
                device_id_type=MESH,
            )
            copy.start()
            started.append(copy)

    def arrive(first_slot, count, recv):
        blocks = ups_ref.at[pl.ds(first_slot, count)]
        pltpu.make_async_copy(blocks, blocks, block_recv.at[recv]).wait()

    def place_in(n):
        return n if groups == 4 else order.index((groups - order[n]) % groups)

    def spread(n):
        send(pair, n, row_peers[:-1] if n in around else row_peers, groups + n)
        send(pair, n, [partner], 2 * groups + n)

    for n in range(1, groups):
        send(pair, 0, [columns[n - 1]], place_in(n))
        if n == 1:
            spread(0)


    def keep_coarse():
        await_load("coarse")
        pre_v[...] = product(coarse_v[...], weight("coarse_w1"))

    def keep_message():
        message_v[...] = product(weight("w_coarse"), weight("coarse_w2")).astype(bf16)

    def fill_table():
        @pl.when(tile > 0)
        def _():
            for copy in to_after[1:]:
                copy.wait_recv()

        @pl.when(tile < tiles - 1)
        def _():
            for copy in to_before[1:]:
                copy.wait_recv()

        table_v[:features, fines : fines + 2 * rims] = flipped(flip_v[0], rim_ref[...]).astype(bf16)
        far = jnp.concatenate([rim_parent_ref[0], rim_parent_ref[1]], axis=1)
        far = jnp.where(far < 0, -1, far - (me - 2) * mids)
        source_parent = jnp.concatenate([own_near + mids, far], axis=1)
        line = lax.broadcasted_iota(i32, (table_v.shape[0] - features, sources), 0)
        table_v[features:, :sources] = jnp.where(line == 0, source_parent, 0).astype(f32).astype(bf16)
        lift_v[...] = one_hot(as_columns(own_near, lift_v.shape[1]), 1, lift_v.shape)

    blocks_of_edges = iter(range(edges // step))

    def do_known(n=1):
        for i in [i for _, i in zip(range(n), blocks_of_edges)]:
            known(i)

    def coarse_part(pieces):
        places = [(heights[n], c) for n, c in pieces]
        blocks = [ups_ref[pl.ds(place_of(h, 0, c), pairs)].reshape(pairs * mids, features) for h, c in places]
        slots = [id_place_of(h, p, c) for h, c in places for p in range(pairs)]
        id_row = jnp.concatenate([ids_ref[slot][:, :mids] for slot in slots], axis=1)
        picker = one_hot(id_row, 0, (coarse_count, len(slots) * mids))
        return product(picker, jnp.concatenate(blocks, axis=0))

    nearby = []
    for d in range(-2, 3):
        other = (me + d + 2 * groups * tiles) % (groups * tiles)
        other_tile = other % tiles
        nearby.append((other // tiles, other_tile // 2, other_tile % 2))

    def find_near():
        window, padded = pick_v.shape
        spare = ceil(window) - window
        near_row = jnp.concatenate([ids_ref[id_place_of(*place)][:, :mids] for place in nearby] + [jnp.zeros((1, spare), i32)], axis=1)
        pick_v[...] = one_hot(as_columns(near_row, padded)[:window], 1, (window, padded))

    def column_rows(place):
        return ups_ref[pl.ds(place, groups)].reshape(groups * mids, features)

    def column_at(n):
        arrive(place_of(heights[n], pair, core), 1, n)
        spread(n)

    def across_at(n):
        here = level[:-1] if n in around else level
        arrive(0, len(here), groups + n)
        if n == 0:
            for m in around:
                send(level[-1], 0, [columns[m - 1]], 3 * groups + m)
        for other in here:
            send(other, n, [partner], 2 * groups + n)

    def corner_at(n):
        arrive(0, 1, 3 * groups + n)
        send(level[-1], n, [partner], 2 * groups + n)

    def partner_at(n):
        arrive(place_of(heights[n], 0, 1 - core), pairs, 2 * groups + n)

    columns_left = iter(range(1, groups))
    across_left = iter(range(groups))

    def relay(left, step_at, n=1):
        for i in [i for _, i in zip(range(n), left)]:
            step_at(i)

    keep_message()
    ids_across()
    fill_table()
    do_known(2)
    relay(columns_left, column_at)
    keep_coarse()
    relay(columns_left, column_at)
    relay(across_left, across_at)
    relay(columns_left, column_at, groups)
    ids_partner()
    do_known(3)
    relay(across_left, across_at)
    relay(across_left, across_at, groups - 3)
    for n in around[:-1]:
        corner_at(n)
    ids_done()
    find_near()
    gained_v[...] = coarse_part([(n, core) for n in range(groups - 1)])
    relay(across_left, across_at, groups)
    for n in around[-1:]:
        corner_at(n)
    do_known(edges)
    for n in range(groups):
        partner_at(n)
    gained_v[...] += coarse_part([(groups - 1, core)] + [(n, 1 - core) for n in range(groups)])
    near_v[...] = jnp.concatenate([ups_ref[place_of(*place)] for place in nearby], axis=0)

    @pl.when(tile > 0)
    def _():
        for copy in to_before:
            copy.wait_send()

    @pl.when(tile < tiles - 1)
    def _():
        for copy in to_after:
            copy.wait_send()

    total = sum(ids_sent)
    for first in range(0, total, ids_ref.shape[0]):
        sent = ids_ref.at[pl.ds(0, min(total - first, ids_ref.shape[0]))]
        pltpu.make_async_copy(sent, sent, id_send.at[0]).wait()
    for first in range(0, len(started), ups_ref.shape[0]):
        blocks = ups_ref.at[pl.ds(0, min(len(started) - first, ups_ref.shape[0]))]
        pltpu.make_async_copy(blocks, blocks, tree_send.at[0]).wait()
    await_load("handed")


def finish_kernel(*refs):
    pre_v, known_v, lookup_v, target_v, fine_v, coarse_v = refs[:6]
    near_v, pick_v, lift_v, flip_v, handed_v, message_v, gained_v = refs[6:13]
    fine_out_ref, mid_out_ref, coarse_out_ref = refs[13:16]
    fine_out_v, mid_out_v, coarse_out_v, padded_v, sums_v, first_v, ending_v, out_sem = refs[16:]
    window, padded = pick_v.shape
    mids = mid_out_v.shape[0]
    fines, features = fine_v.shape
    coarse_count = coarse_v.shape[0]
    edges = known_v.shape[1]
    weights = {name: handed_v.at[i] for i, name in enumerate(FINISH_WEIGHTS)}
    outs = []

    def put(source, target):
        outs.append(pltpu.make_async_copy(source, target, out_sem.at[len(outs)]))
        outs[-1].start()

    quarter = features // 4
    fills = iter(range(8))

    def fill(n=1):
        for i in [i for _, i in zip(range(n), fills)]:
            part = slice(i % 4 * quarter, (i % 4 + 1) * quarter)
            if i < 4:
                ending_v[part] = product(weights["edge_w2"][part], weights["node_w2"][...]).astype(bf16)
            else:
                rows = slice(i % 4 * fines // 4, (i % 4 + 1) * fines // 4)
                first_v[rows] = product(fine_v[rows], weights["node_w1"][...])

    message = product(gained_v[...].astype(bf16), message_v[...])
    fill(2)
    hidden = gate(pre_v[...] + message).astype(bf16)
    change_out = product(hidden, weights["coarse_w3"][...])
    fill(2)
    updated = (coarse_v[...].astype(f32) + normed(change_out)).astype(bf16)
    coarse_out_v[...] = updated
    put(coarse_out_v, coarse_out_ref)
    edge = coarse_count // 16 * 16
    padded_v[edge:] = jnp.zeros((padded - edge, features), bf16)
    padded_v[:coarse_count] = updated

    picked = product(pick_v[...], padded_v[...]).astype(bf16)
    fill()
    down = product(picked, weights["w_descend"][...])
    fill()
    near_out = (near_v[...].astype(f32) + down).astype(bf16)
    mid_out_v[...] = near_out[2 * mids : 3 * mids]
    put(mid_out_v, mid_out_ref)
    fine_down = product(near_out, weights["w_fine"][...]).astype(bf16)
    fill(8)
    beside = fine_down[mids : 4 * mids]

    def blank(rows):
        return jnp.zeros((rows, features), bf16)

    source_rows = jnp.concatenate([fine_down, blank(3 * mids)], axis=0)
    target_rows = jnp.concatenate([blank(5 * mids), beside], axis=0)
    change = (flipped(flip_v[0], source_rows) + flipped(flip_v[1], target_rows)).astype(bf16)

    step = next(size for size in (1024, 512, 256, 128) if edges % size == 0)
    spare = lift_v.shape[1] - 3 * mids
    beside_first = product(beside, weights["node_w1"][...]).astype(bf16)
    lift = lift_v[...]
    if spare:
        beside = jnp.concatenate([beside, blank(spare)], axis=0)
        beside_first = jnp.concatenate([beside_first, blank(spare)], axis=0)
    lifted = (fine_v[...].astype(f32) + product(lift, beside)).astype(bf16)
    incoming = first_v[...] + product(lift, beside_first)
    total = None
    for i in range(edges // step):
        span = slice(i * step, (i + 1) * step)
        edge_sum = product(change, lookup_v[:, span]) + known_v[:, span].astype(f32)
        part = flipped(target_v[:, span], gate(edge_sum).astype(bf16))
        if i == 0:
            sums_v[...] = part
        else:
            sums_v[...] += part

    incoming += product(sums_v[...].astype(bf16), ending_v[...])
    hidden = gate(incoming).astype(bf16)
    cut = fines - ceil(fines // 4, 16)
    for span in (slice(0, cut), slice(cut, fines)):
        result = lifted[span].astype(f32) + normed(product(hidden[span], weights["node_w3"][...]))
        fine_out_v[span] = result.astype(bf16)
        put(fine_out_v.at[span], fine_out_ref.at[span])
    for copy in outs:
        copy.wait()


def on_device(
    fine_latent,
    mid_latent,
    coarse_latent,
    fine_parent,
    mid_parent,
    halo_rows,
    edge_source,
    edge_target,
    w_child,
    mid_w1,
    mid_w2,
    mid_w3,
    w_coarse,
    coarse_w1,
    coarse_w2,
    coarse_w3,
    w_descend,
    w_fine,
    edge_w_src,
    edge_w_dst,
    edge_w2,
    node_w1,
    node_w2,
    node_w3,
):
    named = dict(
        w_child=w_child,
        mid_w1=mid_w1,
        mid_w2=mid_w2,
        mid_w3=mid_w3,
        w_coarse=w_coarse,
        coarse_w1=coarse_w1,
        coarse_w2=coarse_w2,
        coarse_w3=coarse_w3,
        w_descend=w_descend,
        w_fine=w_fine,
        edge_w_src=edge_w_src,
        edge_w_dst=edge_w_dst,
        edge_w2=edge_w2,
        node_w1=node_w1,
        node_w2=node_w2,
        node_w3=node_w3,
    )
    groups, tiles = (lax.axis_size("rhombus"), lax.axis_size("tile"))
    devices = groups * tiles
    fines, features = fine_latent.shape
    mids = mid_latent.shape[0]
    halos = halo_rows.shape[0]
    rims = halos // 2
    edges = edge_source.shape[0]
    coarse_count = coarse_latent.shape[0]
    width = ceil(mids)
    pairs = tiles // 2
    vmem = pl.BlockSpec(memory_space=pltpu.VMEM)
    hbm = pl.BlockSpec(memory_space=pl.ANY)
    dma = pltpu.SemaphoreType.DMA
    square = (features, features)
    small = [fine_parent[None, :], halo_rows[None, :], mid_parent[None, :], mid_latent]
    edge_ids = [edge_source[None, :], edge_target[None, :]]
    weights = [named[name] for name in GATHER_WEIGHTS + FINISH_WEIGHTS]
    handed = (
        pltpu.VMEM((coarse_count, features), f32),
        pltpu.VMEM((features, edges), bf16),
        pltpu.VMEM((8 * mids, edges), bf16),
        pltpu.VMEM((fines, edges), bf16),
        pltpu.VMEM((fines, features), bf16),
        pltpu.VMEM((coarse_count, features), bf16),
        pltpu.VMEM((5 * mids, features), bf16),
        pltpu.VMEM((5 * mids, ceil(coarse_count)), bf16),
        pltpu.VMEM((fines, ceil(3 * mids)), bf16),
        pltpu.VMEM((2, *square), bf16),
        pltpu.VMEM((len(FINISH_WEIGHTS), *square), bf16),
        pltpu.VMEM(square, bf16),
        pltpu.VMEM((coarse_count, features), f32),
    )
    between = pl.pallas_call(
        lambda *refs: gather_kernel(groups, tiles, *refs),
        out_shape=handed,
        in_specs=[hbm] * (len(small) + 4 + len(weights)),
        out_specs=(vmem,) * len(handed),
        scratch_shapes=[
            pltpu.VMEM((devices, mids, features), bf16),
            pltpu.VMEM((devices, 1, width), i32),
            pltpu.VMEM((halos, features), bf16),
            pltpu.VMEM((2, 1, rims), i32),
            pltpu.VMEM((len(GATHER_WEIGHTS), *square), bf16),
            *[pltpu.VMEM(array.shape, array.dtype) for array in small],
            pltpu.VMEM((2, 1, edges), i32),
            pltpu.VMEM((2, mids, features), bf16),
            pltpu.VMEM((2, mids, features), bf16),
            pltpu.VMEM((halos, features), bf16),
            pltpu.VMEM((2, 1, rims), i32),
            pltpu.VMEM((features + 16, 2 * fines + halos), bf16),
            pltpu.VMEM((1, edges), i32),
            dma((len(small) + 4 + len(LOADS),)),
            dma((6,)),
            dma((6,)),
            dma((1,)),
            dma((4 * groups,)),
            dma((1,)),
            dma((pairs + 1,)),
        ],
        compiler_params=pltpu.CompilerParams(collective_id=0, has_side_effects=True, vmem_limit_bytes=40 << 20),
        name="sweep_gather",
    )(*small, *edge_ids, fine_latent, coarse_latent, *weights)
    return pl.pallas_call(
        finish_kernel,
        out_shape=(
            jax.ShapeDtypeStruct((fines, features), bf16),
            jax.ShapeDtypeStruct((mids, features), bf16),
            jax.ShapeDtypeStruct((coarse_count, features), bf16),
        ),
        in_specs=[vmem] * len(handed),
        out_specs=(hbm,) * 3,
        scratch_shapes=[
            pltpu.VMEM((fines, features), bf16),
            pltpu.VMEM((mids, features), bf16),
            pltpu.VMEM((coarse_count, features), bf16),
            pltpu.VMEM((ceil(coarse_count), features), bf16),
            pltpu.VMEM((fines, features), f32),
            pltpu.VMEM((fines, features), f32),
            pltpu.VMEM(square, bf16),
            dma((6,)),
        ],
        compiler_params=pltpu.CompilerParams(vmem_limit_bytes=24 << 20),
        name="sweep_finish",
    )(*between)


def solution(mesh):
    split, rows, whole = (P(("rhombus", "tile")), P(("rhombus", "tile"), None), P())
    placed = (rows, rows, whole) + (split,) * 5 + (whole,) * 16
    return jax.shard_map(
        on_device,
        mesh=mesh,
        in_specs=placed,
        out_specs=(rows, rows, whole),
        check_vma=False,
    )
```

```python
import jax
import jax.numpy as jnp
from jax import lax
from jax.experimental import pallas as pl
from jax.experimental.pallas import tpu as pltpu
from jax.sharding import PartitionSpec as P

MESH = pl.DeviceIdType.MESH

EPSILON = 1e-05

bf16, f32, i32 = (jnp.bfloat16, jnp.float32, jnp.int32)

ACROSS = (((1,), (1,)), ((), ()))


def product(left, right):
    return jnp.dot(left, right, preferred_element_type=f32)


def flipped(left, right):
    return lax.dot_general(left, right, ACROSS, preferred_element_type=f32)


def normed(values):
    return values / jnp.sqrt(jnp.mean(values * values, axis=-1, keepdims=True) + EPSILON)


def gate(values):
    return values * (0.5 + 0.5 * jnp.tanh(0.5 * values))


def one_hot(ids, axis, shape):
    line = lax.broadcasted_iota(jnp.int16, shape, axis)
    return jnp.where(line == ids.astype(jnp.int16), jnp.ones((), bf16), jnp.zeros((), bf16))


def as_columns(row, width):
    count = row.shape[1]
    column = jnp.transpose(jnp.broadcast_to(row, (128, count)))
    return jnp.concatenate([column] * (width // 128), axis=1)


def ceil(n, unit=128):
    return -(-n // unit) * unit


GATHER_WEIGHTS = (
    "w_child",
    "mid_w2",
    "mid_w1",
    "mid_w3",
    "edge_w_dst",
    "edge_w_src",
    "w_coarse",
    "coarse_w2",
    "coarse_w1",
)
FINISH_WEIGHTS = ("coarse_w3", "edge_w2", "node_w2", "w_descend", "w_fine", "node_w1", "node_w3")
EARLY = 0
BY_HEIGHT = (1, 2, 3)
SMALL = ("parent", "halo", "coarse_id", "latent")
LOADS = (2, 2, 1, 1, 2, 1)


def gather_kernel(groups, tiles, *refs):
    refs = iter(refs)

    def take(n):
        return [next(refs) for _ in range(n)]

    small_refs = dict(zip(SMALL + ("source", "target"), take(len(SMALL) + 2)))
    fine_ref, coarse_ref = take(2)
    weight_refs = dict(zip(GATHER_WEIGHTS + FINISH_WEIGHTS, take(len(GATHER_WEIGHTS + FINISH_WEIGHTS))))
    pre_v, known_v, lookup_v, target_v, fine_v, coarse_v = take(6)
    near_v, pick_v, lift_v, flip_v, handed_v, message_v, gained_v = take(7)
    ups_ref, ids_ref, rim_ref, rim_parent_ref, weights_v = take(5)
    small_v = dict(zip(SMALL, take(len(SMALL))))
    (edge_ids_v,) = take(1)
    side_v, beside_v, picked_v, picked_parent_v, table_v, target_near_v = take(6)
    load_sem, near_send, near_recv, tree_send, block_recv, id_send, id_recv = take(7)

    group, tile = (lax.axis_index("rhombus"), lax.axis_index("tile"))
    pairs = tiles // 2
    pair, core = (tile // 2, tile % 2)
    mids = small_v["latent"].shape[0]
    rims = small_v["halo"].shape[1] // 2
    fines, features = fine_v.shape
    coarse_count = coarse_v.shape[0]
    edges = edge_ids_v.shape[2]

    def at(group_id, pair_id, core_id):
        return (group_id, pair_id * 2 + core_id)

    if groups == 4:
        heights = [group, group + 1 - 2 * (group % 2), (group + 2) % 4, 3 - group]
    else:
        order = [0] + sorted(range(1, groups), key=lambda k: min(k, groups - k))
        heights = [(group + k) % groups for k in order]
    columns = [at(height, pair, core) for height in heights[1:]]
    if pairs == 4:
        beside = pair + 1 - 2 * (pair % 2)
        level = [beside, (pair + 2) % 4, (beside + 2) % 4]
        around = BY_HEIGHT if groups == 4 else ()
    else:
        level = [(pair + k) % pairs for k in range(1, pairs)]
        around = ()
    row_peers = [at(group, other, core) for other in level]
    partner = at(group, pair, 1 - core)
    peers = columns + row_peers + [partner]

    barrier = pltpu.get_barrier_semaphore()
    for peer in peers:
        pl.semaphore_signal(barrier, inc=1, device_id=peer, device_id_type=MESH)

    @pl.when(tile > 0)
    def _():
        pl.semaphore_signal(barrier, inc=1, device_id=(group, tile - 1), device_id_type=MESH)

    @pl.when(tile < tiles - 1)
    def _():
        pl.semaphore_signal(barrier, inc=1, device_id=(group, tile + 1), device_id_type=MESH)

    loads = {}

    def load(name, *pairs_of_refs, whole=None):
        sem = load_sem.at[len(loads)]
        for source, held in pairs_of_refs:
            pltpu.make_async_copy(source, held, sem).start()
        held = pairs_of_refs[0][1] if whole is None else whole
        loads[name] = pltpu.make_async_copy(held, held, sem)

    load("parent", (small_refs["parent"], small_v["parent"]))
    load("fine", (fine_ref, fine_v))
    for name in ("halo", "latent", "coarse_id"):
        load(name, (small_refs[name], small_v[name]))
    held = {name: weights_v.at[i] for i, name in enumerate(GATHER_WEIGHTS)}
    held.update({name: handed_v.at[i] for i, name in enumerate(FINISH_WEIGHTS)})
    first = 0
    for n, count in enumerate(LOADS):
        names = GATHER_WEIGHTS[first : first + count]
        load(n, *[(weight_refs[name], held[name]) for name in names], whole=weights_v.at[pl.ds(first, count)])
        first += count
        if n == 1:
            ids = [(small_refs[name], edge_ids_v.at[i]) for i, name in enumerate(("source", "target"))]
            load("edges", *ids, whole=edge_ids_v)
        if n == 4:
            load("coarse", (coarse_ref, coarse_v))
    load("handed", *[(weight_refs[name], held[name]) for name in FINISH_WEIGHTS], whole=handed_v)
    waited = set()

    def await_load(name):
        if name not in waited:
            loads[name].wait()
            waited.add(name)

    def weight(name):
        place = GATHER_WEIGHTS.index(name)
        await_load(next(n for n in range(len(LOADS)) if place < sum(LOADS[: n + 1])))
        return held[name][...]

    me = group * tiles + tile
    halves = groups * pairs

    def place_of(group_id, pair_id, core_id):
        return core_id * halves + group_id * pairs + pair_id

    def id_place_of(group_id, pair_id, core_id):
        return core_id * halves + pair_id * groups + group_id

    mine = place_of(group, pair, core)
    await_load("parent")
    parents = small_v["parent"][...]
    picker = one_hot(parents, 0, (3 * mids, fines))
    await_load("fine")
    sums = product(picker, fine_v[...])
    side_v[0] = sums[mids : 2 * mids].astype(bf16)
    side_v[1] = sums[2 * mids :].astype(bf16)
    pl.semaphore_wait(barrier, len(peers) + 1 + (tile + tiles - 1) // tiles - (tile + 1) // tiles)

    def near(index, source, target, device):
        return pltpu.make_async_remote_copy(
            src_ref=source,
            dst_ref=target,
            send_sem=near_send.at[index],
            recv_sem=near_recv.at[index],
            device_id=device,
            device_id_type=MESH,
        )

    before, after = ((group, tile - 1), (group, tile + 1))
    to_before = [
        near(0, side_v.at[0], beside_v.at[0], before),
        near(1, picked_v.at[pl.ds(0, rims)], rim_ref.at[pl.ds(rims, rims)], before),
        near(2, picked_parent_v.at[0], rim_parent_ref.at[1], before),
    ]
    to_after = [
        near(3, side_v.at[1], beside_v.at[1], after),
        near(4, picked_v.at[pl.ds(rims, rims)], rim_ref.at[pl.ds(0, rims)], after),
        near(5, picked_parent_v.at[1], rim_parent_ref.at[0], after),
    ]

    @pl.when(tile > 0)
    def _():
        to_before[0].start()

    @pl.when(tile < tiles - 1)
    def _():
        to_after[0].start()

    ids_sent = []

    def pass_ids(first_slot, count, device, kind):
        copy = pltpu.make_async_remote_copy(
            src_ref=ids_ref.at[pl.ds(first_slot, count)],
            dst_ref=ids_ref.at[pl.ds(first_slot, count)],
            send_sem=id_send.at[0],
            recv_sem=id_recv.at[kind],
            device_id=device,
            device_id_type=MESH,
        )
        copy.start()
        ids_sent.append(count)

    def await_ids(first_slot, count, kind):
        held_ids = ids_ref.at[pl.ds(first_slot, count)]
        pltpu.make_async_copy(held_ids, held_ids, id_recv.at[kind]).wait()

    def column_of(pair_id, core_id):
        return id_place_of(0, pair_id, core_id)

    await_load("coarse_id")
    spare_ids = jnp.zeros((1, ids_ref.shape[2] - mids), i32)
    my_id = id_place_of(group, pair, core)
    ids_ref[my_id] = jnp.concatenate([small_v["coarse_id"][...], spare_ids], axis=1)
    for device in columns:
        pass_ids(my_id, 1, device, 0)

    def ids_across():
        await_ids(0, groups - 1, 0)
        for n, device in enumerate(row_peers):
            pass_ids(column_of(pair, core), groups, device, 1 + n)

    def ids_partner():
        for n, other in enumerate(level):
            await_ids(column_of(other, core), groups, 1 + n if pairs == 4 else len(level) - n)
        pass_ids(core * halves, halves, partner, len(level) + 1)

    def ids_done():
        await_ids((1 - core) * halves, halves, len(level) + 1)

    await_load("halo")
    halo = small_v["halo"][...]
    picked_v[...] = product(one_hot(as_columns(halo, fines), 1, (2 * rims, fines)), fine_v[...]).astype(bf16)
    side = parents // mids
    shift = jnp.where(side == 1, -1, jnp.where(side == 2, 1, 0))
    within = parents % mids
    parent_column = jnp.transpose(jnp.broadcast_to((me + shift) * mids + within, (128, fines)))
    for half in range(2):
        hit = lax.broadcasted_iota(i32, (fines, rims), 0) == halo[:, half * rims : (half + 1) * rims]
        spread = jnp.concatenate([parent_column] * (rims // 128), axis=1)
        picked_parent_v[half] = jnp.sum(jnp.where(hit, spread, 0), axis=0, keepdims=True)

    @pl.when(tile > 0)
    def _():
        to_before[1].start()
        to_before[2].start()

    @pl.when(tile < tiles - 1)
    def _():
        to_after[1].start()
        to_after[2].start()

    child_mid = product(weight("w_child"), weight("mid_w2")).astype(bf16)
    await_load("latent")
    kept_mid = product(small_v["latent"][...], weight("mid_w1"))
    flip_v[1] = jnp.transpose(weight("edge_w_dst"))
    table_v[:features, fines + 2 * rims :] = flipped(flip_v[1], fine_v[...]).astype(bf16)
    flip_v[0] = jnp.transpose(weight("edge_w_src"))
    table_v[:features, :fines] = flipped(flip_v[0], fine_v[...]).astype(bf16)
    own_near = (1 + shift) * mids + within
    step = next(size for size in (512, 256, 128) if edges % size == 0)
    sources = fines + 2 * rims
    line = lax.broadcasted_iota(i32, (table_v.shape[0] - features, fines), 0)
    table_v[features:, sources:] = jnp.where(line == 1, own_near, 0).astype(f32).astype(bf16)

    def known_target(i):
        span = pl.ds(i * step, step)
        target_pick = one_hot(edge_ids_v[1, :, span], 0, (fines, step))
        target_v[:, span] = target_pick
        found = product(table_v[:, sources:], target_pick)
        known_v[:, span] = found[:features].astype(bf16)
        target_near_v[:, span] = found[features + 1 : features + 2].astype(i32)

    def known(i):
        span = pl.ds(i * step, step)
        source_pick = one_hot(edge_ids_v[0, :, span], 0, (sources, step))
        if i < EARLY:
            found = product(table_v[:, :sources], source_pick)
            known_v[:, span] = (found[:features] + known_v[:, span].astype(f32)).astype(bf16)
            target_near = target_near_v[:, span]
        else:
            target_pick = one_hot(edge_ids_v[1, :, span], 0, (fines, step))
            target_v[:, span] = target_pick
            found = product(table_v[...], jnp.concatenate([source_pick, target_pick], axis=0))
            known_v[:, span] = found[:features].astype(bf16)
            target_near = found[features + 1 : features + 2].astype(i32)
        source_near = found[features : features + 1].astype(i32)
        line = lax.broadcasted_iota(i32, (8 * mids, step), 0)
        hit = (line == source_near) | (line == target_near + 5 * mids)
        lookup_v[:, span] = jnp.where(hit, 1.0, 0.0).astype(bf16)

    await_load("edges")
    for i in range(EARLY):
        known_target(i)
    mid_w3 = weight("mid_w3")

    @pl.when(tile > 0)
    def _():
        to_after[0].wait_recv()

    @pl.when(tile == 0)
    def _():
        beside_v[1] = jnp.zeros_like(beside_v[1])
        rim_ref[pl.ds(0, rims)] = jnp.zeros((rims, features), bf16)
        rim_parent_ref[0] = jnp.full(rim_parent_ref.shape[1:], -1, i32)

    @pl.when(tile < tiles - 1)
    def _():
        to_before[0].wait_recv()

    @pl.when(tile == tiles - 1)
    def _():
        beside_v[0] = jnp.zeros_like(beside_v[0])
        rim_ref[pl.ds(rims, rims)] = jnp.zeros((rims, features), bf16)
        rim_parent_ref[1] = jnp.full(rim_parent_ref.shape[1:], -1, i32)

    total = (sums[:mids] + beside_v[0].astype(f32) + beside_v[1].astype(f32)).astype(bf16)
    hidden = gate(kept_mid + product(total, child_mid)).astype(bf16)
    mid_up = small_v["latent"][...].astype(f32) + normed(product(hidden, mid_w3))
    ups_ref[mine] = mid_up.astype(bf16)

    started = []

    def send(pair_id, n, devices, recv):
        slot = place_of(heights[n], pair_id, core)
        for device in devices:
            copy = pltpu.make_async_remote_copy(
                src_ref=ups_ref.at[slot],
                dst_ref=ups_ref.at[slot],
                send_sem=tree_send.at[0],
                recv_sem=block_recv.at[recv],
                device_id=device,
                device_id_type=MESH,
            )
            copy.start()
            started.append(copy)

    def arrive(first_slot, count, recv):
        blocks = ups_ref.at[pl.ds(first_slot, count)]
        pltpu.make_async_copy(blocks, blocks, block_recv.at[recv]).wait()

    def place_in(n):
        return n if groups == 4 else order.index((groups - order[n]) % groups)

    def spread(n):
        send(pair, n, row_peers[:-1] if n in around else row_peers[::-1], groups + n)
        send(pair, n, [partner], 2 * groups + n)

    for n in range(1, groups):
        send(pair, 0, [columns[n - 1]], place_in(n))
        if n == 1:
            spread(0)


    def keep_coarse():
        await_load("coarse")
        pre_v[...] = product(coarse_v[...], weight("coarse_w1"))

    def keep_message():
        message_v[...] = product(weight("w_coarse"), weight("coarse_w2")).astype(bf16)

    def fill_table():
        @pl.when(tile > 0)
        def _():
            for copy in to_after[1:]:
                copy.wait_recv()

        @pl.when(tile < tiles - 1)
        def _():
            for copy in to_before[1:]:
                copy.wait_recv()

        table_v[:features, fines : fines + 2 * rims] = flipped(flip_v[0], rim_ref[...]).astype(bf16)
        far = jnp.concatenate([rim_parent_ref[0], rim_parent_ref[1]], axis=1)
        far = jnp.where(far < 0, -1, far - (me - 2) * mids)
        source_parent = jnp.concatenate([own_near + mids, far], axis=1)
        line = lax.broadcasted_iota(i32, (table_v.shape[0] - features, sources), 0)
        table_v[features:, :sources] = jnp.where(line == 0, source_parent, 0).astype(f32).astype(bf16)
        lift_v[...] = one_hot(as_columns(own_near, lift_v.shape[1]), 1, lift_v.shape)

    blocks_of_edges = iter(range(edges // step))

    def do_known(n=1):
        for i in [i for _, i in zip(range(n), blocks_of_edges)]:
            known(i)

    def coarse_part(pieces):
        places = [(heights[n], c) for n, c in pieces]
        blocks = [ups_ref[pl.ds(place_of(h, 0, c), pairs)].reshape(pairs * mids, features) for h, c in places]
        slots = [id_place_of(h, p, c) for h, c in places for p in range(pairs)]
        id_row = jnp.concatenate([ids_ref[slot][:, :mids] for slot in slots], axis=1)
        picker = one_hot(id_row, 0, (coarse_count, len(slots) * mids))
        return product(picker, jnp.concatenate(blocks, axis=0))

    nearby = []
    for d in range(-2, 3):
        other = (me + d + 2 * groups * tiles) % (groups * tiles)
        other_tile = other % tiles
        nearby.append((other // tiles, other_tile // 2, other_tile % 2))

    def find_near():
        window, padded = pick_v.shape
        spare = ceil(window) - window
        near_row = jnp.concatenate([ids_ref[id_place_of(*place)][:, :mids] for place in nearby] + [jnp.zeros((1, spare), i32)], axis=1)
        pick_v[...] = one_hot(as_columns(near_row, padded)[:window], 1, (window, padded))

    def column_rows(place):
        return ups_ref[pl.ds(place, groups)].reshape(groups * mids, features)

    def column_at(n):
        arrive(place_of(heights[n], pair, core), 1, n)
        spread(n)

    def across_at(n):
        here = level[:-1] if n in around else level
        arrive(0, len(here), groups + n)
        if n == 0:
            for m in around:
                send(level[-1], 0, [columns[m - 1]], 3 * groups + m)
        for other in here:
            send(other, n, [partner], 2 * groups + n)

    def corner_at(n):
        arrive(0, 1, 3 * groups + n)
        send(level[-1], n, [partner], 2 * groups + n)

    def partner_at(n):
        arrive(place_of(heights[n], 0, 1 - core), pairs, 2 * groups + n)

    columns_left = iter(range(1, groups))
    across_left = iter(range(groups))

    def relay(left, step_at, n=1):
        for i in [i for _, i in zip(range(n), left)]:
            step_at(i)

    keep_message()
    ids_across()
    fill_table()
    do_known(2)
    relay(columns_left, column_at)
    keep_coarse()
    relay(columns_left, column_at)
    relay(across_left, across_at)
    relay(columns_left, column_at, groups)
    ids_partner()
    do_known(3)
    relay(across_left, across_at)
    relay(across_left, across_at, groups - 3)
    for n in around[:-1]:
        corner_at(n)
    ids_done()
    find_near()
    gained_v[...] = coarse_part([(n, core) for n in range(groups - 1)])
    relay(across_left, across_at, groups)
    for n in around[-1:]:
        corner_at(n)
    do_known(edges)
    for n in range(groups):
        partner_at(n)
    gained_v[...] += coarse_part([(groups - 1, core)] + [(n, 1 - core) for n in range(groups)])
    near_v[...] = jnp.concatenate([ups_ref[place_of(*place)] for place in nearby], axis=0)

    @pl.when(tile > 0)
    def _():
        for copy in to_before:
            copy.wait_send()

    @pl.when(tile < tiles - 1)
    def _():
        for copy in to_after:
            copy.wait_send()

    total = sum(ids_sent)
    for first in range(0, total, ids_ref.shape[0]):
        sent = ids_ref.at[pl.ds(0, min(total - first, ids_ref.shape[0]))]
        pltpu.make_async_copy(sent, sent, id_send.at[0]).wait()
    for first in range(0, len(started), ups_ref.shape[0]):
        blocks = ups_ref.at[pl.ds(0, min(len(started) - first, ups_ref.shape[0]))]
        pltpu.make_async_copy(blocks, blocks, tree_send.at[0]).wait()
    await_load("handed")


def finish_kernel(*refs):
    pre_v, known_v, lookup_v, target_v, fine_v, coarse_v = refs[:6]
    near_v, pick_v, lift_v, flip_v, handed_v, message_v, gained_v = refs[6:13]
    fine_out_ref, mid_out_ref, coarse_out_ref = refs[13:16]
    fine_out_v, mid_out_v, coarse_out_v, padded_v, sums_v, first_v, ending_v, out_sem = refs[16:]
    window, padded = pick_v.shape
    mids = mid_out_v.shape[0]
    fines, features = fine_v.shape
    coarse_count = coarse_v.shape[0]
    edges = known_v.shape[1]
    weights = {name: handed_v.at[i] for i, name in enumerate(FINISH_WEIGHTS)}
    outs = []

    def put(source, target):
        outs.append(pltpu.make_async_copy(source, target, out_sem.at[len(outs)]))
        outs[-1].start()

    quarter = features // 4
    fills = iter(range(8))

    def fill(n=1):
        for i in [i for _, i in zip(range(n), fills)]:
            part = slice(i % 4 * quarter, (i % 4 + 1) * quarter)
            if i < 4:
                ending_v[part] = product(weights["edge_w2"][part], weights["node_w2"][...]).astype(bf16)
            else:
                rows = slice(i % 4 * fines // 4, (i % 4 + 1) * fines // 4)
                first_v[rows] = product(fine_v[rows], weights["node_w1"][...])

    message = product(gained_v[...].astype(bf16), message_v[...])
    fill(2)
    hidden = gate(pre_v[...] + message).astype(bf16)
    change_out = product(hidden, weights["coarse_w3"][...])
    fill(2)
    updated = (coarse_v[...].astype(f32) + normed(change_out)).astype(bf16)
    coarse_out_v[...] = updated
    put(coarse_out_v, coarse_out_ref)
    edge = coarse_count // 16 * 16
    padded_v[edge:] = jnp.zeros((padded - edge, features), bf16)
    padded_v[:coarse_count] = updated

    picked = product(pick_v[...], padded_v[...]).astype(bf16)
    fill()
    down = product(picked, weights["w_descend"][...])
    fill()
    near_out = (near_v[...].astype(f32) + down).astype(bf16)
    mid_out_v[...] = near_out[2 * mids : 3 * mids]
    put(mid_out_v, mid_out_ref)
    fine_down = product(near_out, weights["w_fine"][...]).astype(bf16)
    fill(8)
    beside = fine_down[mids : 4 * mids]

    def blank(rows):
        return jnp.zeros((rows, features), bf16)

    source_rows = jnp.concatenate([fine_down, blank(3 * mids)], axis=0)
    target_rows = jnp.concatenate([blank(5 * mids), beside], axis=0)
    change = (flipped(flip_v[0], source_rows) + flipped(flip_v[1], target_rows)).astype(bf16)

    step = next(size for size in (1024, 512, 256, 128) if edges % size == 0)
    spare = lift_v.shape[1] - 3 * mids
    beside_first = product(beside, weights["node_w1"][...]).astype(bf16)
    lift = lift_v[...]
    if spare:
        beside = jnp.concatenate([beside, blank(spare)], axis=0)
        beside_first = jnp.concatenate([beside_first, blank(spare)], axis=0)
    lifted = (fine_v[...].astype(f32) + product(lift, beside)).astype(bf16)
    incoming = first_v[...] + product(lift, beside_first)
    total = None
    for i in range(edges // step):
        span = slice(i * step, (i + 1) * step)
        edge_sum = product(change, lookup_v[:, span]) + known_v[:, span].astype(f32)
        part = flipped(target_v[:, span], gate(edge_sum).astype(bf16))
        if i == 0:
            sums_v[...] = part
        else:
            sums_v[...] += part

    incoming += product(sums_v[...].astype(bf16), ending_v[...])
    hidden = gate(incoming).astype(bf16)
    cut = fines - ceil(fines // 4, 16)
    for span in (slice(0, cut), slice(cut, fines)):
        result = lifted[span].astype(f32) + normed(product(hidden[span], weights["node_w3"][...]))
        fine_out_v[span] = result.astype(bf16)
        put(fine_out_v.at[span], fine_out_ref.at[span])
    for copy in outs:
        copy.wait()


def on_device(
    fine_latent,
    mid_latent,
    coarse_latent,
    fine_parent,
    mid_parent,
    halo_rows,
    edge_source,
    edge_target,
    w_child,
    mid_w1,
    mid_w2,
    mid_w3,
    w_coarse,
    coarse_w1,
    coarse_w2,
    coarse_w3,
    w_descend,
    w_fine,
    edge_w_src,
    edge_w_dst,
    edge_w2,
    node_w1,
    node_w2,
    node_w3,
):
    named = dict(
        w_child=w_child,
        mid_w1=mid_w1,
        mid_w2=mid_w2,
        mid_w3=mid_w3,
        w_coarse=w_coarse,
        coarse_w1=coarse_w1,
        coarse_w2=coarse_w2,
        coarse_w3=coarse_w3,
        w_descend=w_descend,
        w_fine=w_fine,
        edge_w_src=edge_w_src,
        edge_w_dst=edge_w_dst,
        edge_w2=edge_w2,
        node_w1=node_w1,
        node_w2=node_w2,
        node_w3=node_w3,
    )
    groups, tiles = (lax.axis_size("rhombus"), lax.axis_size("tile"))
    devices = groups * tiles
    fines, features = fine_latent.shape
    mids = mid_latent.shape[0]
    halos = halo_rows.shape[0]
    rims = halos // 2
    edges = edge_source.shape[0]
    coarse_count = coarse_latent.shape[0]
    width = ceil(mids)
    pairs = tiles // 2
    vmem = pl.BlockSpec(memory_space=pltpu.VMEM)
    hbm = pl.BlockSpec(memory_space=pl.ANY)
    dma = pltpu.SemaphoreType.DMA
    square = (features, features)
    small = [fine_parent[None, :], halo_rows[None, :], mid_parent[None, :], mid_latent]
    edge_ids = [edge_source[None, :], edge_target[None, :]]
    weights = [named[name] for name in GATHER_WEIGHTS + FINISH_WEIGHTS]
    handed = (
        pltpu.VMEM((coarse_count, features), f32),
        pltpu.VMEM((features, edges), bf16),
        pltpu.VMEM((8 * mids, edges), bf16),
        pltpu.VMEM((fines, edges), bf16),
        pltpu.VMEM((fines, features), bf16),
        pltpu.VMEM((coarse_count, features), bf16),
        pltpu.VMEM((5 * mids, features), bf16),
        pltpu.VMEM((5 * mids, ceil(coarse_count)), bf16),
        pltpu.VMEM((fines, ceil(3 * mids)), bf16),
        pltpu.VMEM((2, *square), bf16),
        pltpu.VMEM((len(FINISH_WEIGHTS), *square), bf16),
        pltpu.VMEM(square, bf16),
        pltpu.VMEM((coarse_count, features), f32),
    )
    between = pl.pallas_call(
        lambda *refs: gather_kernel(groups, tiles, *refs),
        out_shape=handed,
        in_specs=[hbm] * (len(small) + 4 + len(weights)),
        out_specs=(vmem,) * len(handed),
        scratch_shapes=[
            pltpu.VMEM((devices, mids, features), bf16),
            pltpu.VMEM((devices, 1, width), i32),
            pltpu.VMEM((halos, features), bf16),
            pltpu.VMEM((2, 1, rims), i32),
            pltpu.VMEM((len(GATHER_WEIGHTS), *square), bf16),
            *[pltpu.VMEM(array.shape, array.dtype) for array in small],
            pltpu.VMEM((2, 1, edges), i32),
            pltpu.VMEM((2, mids, features), bf16),
            pltpu.VMEM((2, mids, features), bf16),
            pltpu.VMEM((halos, features), bf16),
            pltpu.VMEM((2, 1, rims), i32),
            pltpu.VMEM((features + 16, 2 * fines + halos), bf16),
            pltpu.VMEM((1, edges), i32),
            dma((len(small) + 4 + len(LOADS),)),
            dma((6,)),
            dma((6,)),
            dma((1,)),
            dma((4 * groups,)),
            dma((1,)),
            dma((pairs + 1,)),
        ],
        compiler_params=pltpu.CompilerParams(collective_id=0, has_side_effects=True, vmem_limit_bytes=40 << 20),
        name="sweep_gather",
    )(*small, *edge_ids, fine_latent, coarse_latent, *weights)
    return pl.pallas_call(
        finish_kernel,
        out_shape=(
            jax.ShapeDtypeStruct((fines, features), bf16),
            jax.ShapeDtypeStruct((mids, features), bf16),
            jax.ShapeDtypeStruct((coarse_count, features), bf16),
        ),
        in_specs=[vmem] * len(handed),
        out_specs=(hbm,) * 3,
        scratch_shapes=[
            pltpu.VMEM((fines, features), bf16),
            pltpu.VMEM((mids, features), bf16),
            pltpu.VMEM((coarse_count, features), bf16),
            pltpu.VMEM((ceil(coarse_count), features), bf16),
            pltpu.VMEM((fines, features), f32),
            pltpu.VMEM((fines, features), f32),
            pltpu.VMEM(square, bf16),
            dma((6,)),
        ],
        compiler_params=pltpu.CompilerParams(vmem_limit_bytes=24 << 20),
        name="sweep_finish",
    )(*between)


def solution(mesh):
    split, rows, whole = (P(("rhombus", "tile")), P(("rhombus", "tile"), None), P())
    placed = (rows, rows, whole) + (split,) * 5 + (whole,) * 16
    return jax.shard_map(
        on_device,
        mesh=mesh,
        in_specs=placed,
        out_specs=(rows, rows, whole),
        check_vma=False,
    )
```
